32 devices in a mesh: groups: 2 (over y), tile: 8 (over z, x), cuts: 2 (over core).
Axes of the slice: x: 2, y: 2, z: 4, core: 2. Of those that a mesh axis runs over, the one named last changes fastest.
Arguments:
- slice_rows: float32 [8192, 512], P(('groups', 'tile', 'cuts')), parts along dimension 0, may hold values from -0.025625 to 0.025625
- row_owner: int32 [8192, 1], P(('groups', 'tile', 'cuts')), parts along dimension 0, may hold values from 0 to 7; in each aligned block of 256 rows (0 to 255, 256 to 511, ...) at most 48 rows name the same one
- leaf_row: int32 [8192], P(('groups', 'tile', 'cuts')), parts along dimension 0, may hold values from 0 to 511
- exponent: int32 [8192], P(('groups', 'tile', 'cuts')), parts along dimension 0, may hold values from -1 to 1
- environment: float32 [16384, 512], P(('groups', 'tile', 'cuts')), parts along dimension 0, may hold values from -0.25 to 0.25
- ordering: int32 [32, 512], P(('groups', 'tile', 'cuts')), parts along dimension 0, may hold values from 0 to 511, each once within a row
- sign_mask: int32 [32, 512], P(('groups', 'tile', 'cuts')), parts along dimension 0, may hold values 0 or 1
Outputs:
- partition: float32 [1024, 512], P(('groups', 'tile'), 'cuts'), parts along dimension 0
- log_scale: float32 [2], P('groups'), parts along dimension 0
The draws below stay inside these ranges and needn't reach their ends.
There are 2 independent parts, one for each index of `groups`. The reference program is written for one: setup_inputs(seed, part) draws one part's arguments, and reference() takes and returns one part's arrays. A program takes and returns all parts, laid end to end along the dimension named above; each array names one. Nothing has to cross between parts.
Inputs may be any that keep to these rules, and one draw needn't show every extreme that they name: `row_owner`: of the rows of one device at most 48 name the same owner, and in some device exactly 48 do.
All inputs are finite; a program needn't handle non-finite values. No bound on the sum of `sign_mask` on one device may be relied on, other than what follows from the above.
Results may differ from the reference program's by a relative error of at most 0.0003.
Values sent between devices are 32-bit elements; how exact they have to be, the bound alone decides.
No kernel may reach another device: no remote copies, remote signals or barrier semaphores. Data moves between devices by JAX's collectives and lax.ppermute only.
A program may use at most 64 MiB of HBM per device.

```python
import math
import jax
import jax.numpy as jnp
import numpy as np
from jax import lax

W = 512
ROWS_DEV = 256
CAP = 48
LEAVES = 16
ROWS = 4096
N_TILE = 8
N_CUTS = 2


def place_ends(result, own_key, smallest, top_value):
    longest = result.shape.index(max(result.shape))
    spots = []
    for shift in (0, 1):
        where = [jax.random.randint(jax.random.fold_in(own_key, axis), (), 0, length) for axis, length in enumerate(result.shape)]
        where[longest] = (where[longest] + shift) % result.shape[longest]
        spots.append(tuple(where))
    return result.at[spots[0]].set(smallest).at[spots[1]].set(top_value)


def steps_of(key, dims, shards, low, top_value):
    factor_of = 1.0
    for position, parts in shards:
        draws = jax.random.uniform(jax.random.fold_in(jax.random.fold_in(key, 6), position), (parts,), jnp.float32, low / len(shards), top_value / len(shards))
        factor_of = factor_of * jnp.repeat(jnp.exp(draws), dims[position] // parts).reshape((-1,) + (1,) * (len(dims) - 1 - position))
    return factor_of


def deal_out(own_key, own, number, rows, amount, top, bound, lean):
    sequence = jax.random.permutation(own_key, amount)
    crowded, usual = portions_of(amount, rows * top, bound, lean, True), portions_of(amount, rows * top, bound, lean, False)
    places = jnp.arange(amount)

    def named(tallies, turn):
        used = int((tallies > 0).sum())
        fixed = max(1, used // 4)
        shifted = fixed + (places - fixed + turn * (used - fixed)) % max(1, amount - fixed)
        return jnp.zeros((amount,), jnp.int32).at[sequence[jnp.where(places < fixed, places, shifted)]].set(jnp.asarray(tallies, jnp.int32))

    tallies = jnp.where(number % 4 == 0, named(crowded, number // 4), named(usual, number - number // 4 - 1))
    mixed = jax.random.permutation(jax.random.fold_in(own, 3), amount)
    giver, sink = mixed[0:amount // 2 * 2:2], mixed[1:amount // 2 * 2:2]
    room = jnp.minimum(tallies[giver] - 1, bound - tallies[sink]) // 2
    room = jnp.where((giver == sequence[0]) | (sink == sequence[0]) | (tallies[sink] == 0), 0, jnp.maximum(room, 0))
    shifted = jax.random.randint(jax.random.fold_in(own, 4), (amount // 2,), 0, 1 << 20) % (room + 1)
    tallies = tallies.at[giver].add(-shifted).at[sink].add(shifted)
    labels = jnp.searchsorted(jnp.cumsum(tallies), jnp.arange(rows * top), side="right").astype(jnp.int32)
    listing = labels.reshape(top, rows).T
    listing = listing[jax.random.permutation(jax.random.fold_in(own, 1), rows)]
    turn = jax.random.randint(jax.random.fold_in(own, 2), (rows, 1), 0, top)
    return jnp.take_along_axis(listing, (jnp.arange(top)[None, :] + turn) % top, axis=1)


def portions_of(count, total, limit, lean, full):
    portions = [(1 << 20) // math.isqrt(grade ** lean) + 1 for grade in range(1, count + 1)]
    largest = limit if full else min(limit, max(-(-total // count), total * portions[0] // sum(portions)))
    least = 1 if total - largest >= count - 1 else 0
    given, spare = [largest] + [least] * (count - 1), total - largest - least * (count - 1)
    while spare > 0:
        free = [i for i in range(1, count) if given[i] < largest] or [i for i in range(1, count) if given[i] < limit]
        whole, left = sum([portions[i] for i in free]), spare
        for i in free:
            extra = min(limit - given[i], max(1, left * portions[i] // whole), spare)
            given[i] = given[i] + extra
            spare = spare - extra
    return np.array(given)


def normal_values(rng, extent, scale, bound, pieces=(), held_as=jnp.bfloat16):
    result = scale * jax.random.normal(rng, extent, jnp.float32)
    if pieces:
        result = result * steps_of(rng, extent, pieces, -0.22, 0.18)
    return jnp.clip(result, -bound, bound).astype(held_as)


def setup_inputs(seed: int = 0, part: int = 0) -> dict:
    arg_keys = jax.random.split(jax.random.key(seed), 8)
    own_keys = jax.random.split(jax.random.fold_in(arg_keys[7], part), 8)
    slice_rows = normal_values(own_keys[0], (ROWS, W), (0.068 / ROWS_DEV ** 0.5), 0.025625, ((0, 16),), jnp.float32)
    row_owner_keys = jax.random.split(jax.random.fold_in(own_keys[1], 1), ROWS // ROWS_DEV)
    row_owner_turns = jax.random.permutation(jax.random.fold_in(own_keys[1], 3), ROWS // ROWS_DEV)
    row_owner = jax.vmap(lambda own, number: deal_out(jax.random.fold_in(own_keys[1], 2), own, number, ROWS_DEV, N_TILE, 1, CAP, 2))(row_owner_keys, row_owner_turns).reshape((ROWS, 1))
    leaf_row = place_ends(jax.random.randint(own_keys[2], (ROWS,), 0, W), jax.random.fold_in(own_keys[2], 1), 0, W - 1).astype(jnp.int32)
    exponent = place_ends(jax.random.randint(own_keys[3], (ROWS,), -1, 2), jax.random.fold_in(own_keys[3], 1), -1, 1).astype(jnp.int32)
    environment = normal_values(own_keys[4], (LEAVES * W, W), W ** -0.5, 0.25, ((0, 16),), jnp.float32)
    ordering = jax.vmap(lambda own: jax.random.permutation(own, W))(jax.random.split(own_keys[5], LEAVES)).reshape((LEAVES, W)).astype(jnp.int32)
    sign_mask = place_ends((jax.random.randint(own_keys[6], (LEAVES, W), 0, 2) < 1).astype(jnp.int32), jax.random.fold_in(own_keys[6], 1), 0, 1)
    return {"slice_rows": slice_rows, "row_owner": row_owner, "leaf_row": leaf_row, "exponent": exponent, "environment": environment, "ordering": ordering, "sign_mask": sign_mask}


def reference(slice_rows, row_owner, leaf_row, exponent, environment, ordering, sign_mask):
    leaves = N_TILE * N_CUTS
    width = slice_rows.shape[1]
    source = jnp.arange(slice_rows.shape[0], dtype=jnp.int32) // ROWS_DEV
    target = (row_owner[:, 0] * N_CUTS + source % N_CUTS).astype(jnp.int32)
    factor = jnp.where(exponent == -1, 0.5, jnp.where(exponent == 1, 2.0, 1.0)).astype(jnp.float32)
    scaled = slice_rows * factor[:, None]
    collected = jnp.zeros((leaves, width, width), jnp.float32).at[target, leaf_row].add(scaled)
    environ = environment.reshape(leaves, width, width)
    columns = jnp.arange(width, dtype=jnp.int32)

    def advance(product, ordinal):
        device = ordinal % N_TILE * N_CUTS + ordinal // N_TILE
        contracted = jnp.dot(collected[device], environ[device], precision=lax.Precision.HIGHEST, preferred_element_type=jnp.float32)
        signs = 1.0 - 2.0 * sign_mask[device].astype(jnp.float32)
        signed = (ordering[device][:, None] == columns[None, :]).astype(jnp.float32) * signs[:, None]
        leaf = contracted + signed
        return (jnp.dot(product, leaf, precision=lax.Precision.HIGHEST, preferred_element_type=jnp.float32), None)
    product, _ = lax.scan(advance, jnp.eye(width, dtype=jnp.float32), jnp.arange(leaves, dtype=jnp.int32))
    spread = jnp.sqrt(jnp.mean(product * product) + 1e-06)
    return (product / spread, jnp.log(spread).reshape(1))
```

```python
import functools

import jax
import jax.numpy as jnp
from jax import lax
from jax.experimental import pallas as pl
from jax.experimental.pallas import tpu as pltpu
from jax.sharding import PartitionSpec as P

AXES = ("tile", "cuts")
VMEM = pl.BlockSpec(memory_space=pltpu.VMEM)
BF, F32 = jnp.bfloat16, jnp.float32
PAD = 8


def pairs(tiles, place):
    out = []
    for t in range(tiles):
        for c in range(2):
            to, core = place(t, c)
            out.append((t * 2 + c, to * 2 + core))
    return out


def moved(x, place):
    return lax.ppermute(x, AXES, pairs(lax.axis_size("tile"), place))


def routed(m):
    def place(t, c):
        to = t ^ (m << 1)
        return (to ^ 1, c ^ 1) if (t & 1) == c else (to, c)

    return place


def other_core(t, c):
    return t, c ^ 1


def across(level):
    return lambda t, c: (t ^ (1 << level), c)


def mul(a, b, dims=None):
    if dims is None:
        return jnp.dot(a, b, preferred_element_type=F32)
    return lax.dot_general(a, b, (dims, ((), ())), preferred_element_type=F32)


def split2(x):
    hi = x.astype(BF)
    return hi, (x - hi.astype(F32)).astype(BF)


def split3(x):
    hi = x.astype(BF)
    rest = x - hi.astype(F32)
    mid = rest.astype(BF)
    return hi, mid, (rest - mid.astype(F32)).astype(BF)


def product(a, b):
    ah, al = split2(a)
    bh, bl = split2(b)
    return mul(ah, bh) + (mul(ah, bl) + mul(al, bh))


def call(kernel, outs, args, scratch=(), flops=0):
    size = sum(a.size * 4 for a in args) + sum(o.size * 4 for o in outs)
    return pl.pallas_call(
        kernel,
        out_shape=tuple(outs),
        in_specs=[VMEM] * len(args),
        out_specs=tuple([VMEM] * len(outs)),
        scratch_shapes=list(scratch),
        cost_estimate=pl.CostEstimate(flops=flops, bytes_accessed=size, transcendentals=0),
    )(*args)


def like(*shape):
    return jax.ShapeDtypeStruct(shape, F32)


def pack_kernel(tiles, cap, rows_ref, owner_ref, leaf_ref, exp_ref, order_ref, sign_ref, *outs):
    count = rows_ref.shape[0]
    tile = lax.axis_index("tile")
    own = owner_ref[...]
    hits = own == lax.broadcasted_iota(jnp.int32, (tiles, count), 0)
    earlier = lax.broadcasted_iota(jnp.int32, (count, count), 0) < lax.broadcasted_iota(jnp.int32, (count, count), 1)
    before = mul(jnp.where(hits, 1.0, 0.0).astype(BF), jnp.where(earlier, 1.0, 0.0).astype(BF))
    position = jnp.sum(jnp.where(hits, before, 0.0), axis=0, keepdims=True).astype(jnp.int32)
    placed = (own ^ tile) * cap + position
    power = exp_ref[...]
    factor = jnp.where(power == -1, 0.5, jnp.where(power == 1, 2.0, 1.0))
    row = leaf_ref[...] + 1
    which = lax.broadcasted_iota(jnp.int32, (PAD, count), 0)
    digits = jnp.where(which == 0, row >> 4, jnp.where(which == 1, row & 15, 0)).astype(F32).astype(BF)
    hi, mid, lo = split3(rows_ref[...])
    for m, out in enumerate(outs):
        slots = lax.broadcasted_iota(jnp.int32, (2 * cap, count), 0) + m * 2 * cap
        hot = slots == placed
        pick = jnp.where(hot, factor, 0.0).astype(BF)
        out[0 : 2 * cap, :] = mul(pick, hi) + (mul(pick, mid) + mul(pick, lo))
        out[2 * cap : 2 * cap + PAD, :] = jnp.zeros((PAD, out.shape[1]), F32)
        out[2 * cap : 2 * cap + PAD, 0 : 2 * cap] = mul(digits, jnp.where(hot, 1.0, 0.0).astype(BF), ((1,), (1,)))
    signs = 1 - 2 * sign_ref[...]
    outs[0][2 * cap + 2 : 2 * cap + 3, :] = ((order_ref[...] + 1) * signs).astype(F32)


def leaf_kernel(cap, count, *refs):
    near, far, env_ref, leaf_ref = refs[:count], refs[count : 2 * count], refs[2 * count], refs[2 * count + 1]
    width = env_ref.shape[1]
    eh, el = split2(env_ref[...])
    lane = lax.broadcasted_iota(jnp.int32, (1, 128), 1)
    targets = lax.broadcasted_iota(jnp.int32, (width, 128), 0) + 1
    total = None
    for m in range(0, count, 2):
        spread, chosen = [], []
        for i in (m, m + 1):
            block = jnp.concatenate([near[i][0:cap, :], far[i][cap : 2 * cap, :]], axis=0)
            bh, bl = split2(block)
            spread.append(mul(bh, eh) + (mul(bh, el) + mul(bl, eh)))
            spread.append(jnp.zeros((128 - 2 * cap, width), F32))
            digits = jnp.where(lane < cap, near[i][2 * cap : 2 * cap + PAD, 0:128], far[i][2 * cap : 2 * cap + PAD, 0:128])
            to = (digits[0:1, :] * 16.0 + digits[1:2, :]).astype(jnp.int32)
            to = jnp.where(lane < 2 * cap, to, 0)
            chosen.append(jnp.where(targets == to, 1.0, 0.0).astype(BF))
        sh, sl = split2(jnp.concatenate(spread, axis=0))
        pick = jnp.concatenate(chosen, axis=1)
        part = mul(pick, sh) + mul(pick, sl)
        total = part if total is None else total + part
    code = near[0][2 * cap : 2 * cap + PAD, :]
    column = jnp.transpose(code)[:, 2:3]
    bond = (jnp.abs(column) - 1.0).astype(jnp.int32)
    sign = jnp.where(column < 0.0, -1.0, 1.0)
    spots = lax.broadcasted_iota(jnp.int32, (width, width), 1)
    leaf_ref[...] = total + jnp.where(spots == bond, sign, 0.0)


def half_of(core, value, half_ref):
    size = half_ref.shape[0]
    for k in range(2):

        @pl.when(core == k)
        def _(k=k):
            half_ref[...] = value[k * size : (k + 1) * size, :]


def pair_kernel(own_ref, other_ref, out_ref, half_ref):
    core = lax.axis_index("cuts")

    @pl.when(core == 1)
    def _():
        out_ref[...] = product(own_ref[...], other_ref[...])

    @pl.when(core == 0)
    def _():
        out_ref[...] = product(other_ref[...], own_ref[...])

    half_of(core, out_ref, half_ref)


def combine(bit, left_if, own_ref, near_ref, far_ref, out_ref):
    core = lax.axis_index("cuts")
    left = ((lax.axis_index("tile") >> bit) & 1) == left_if
    size = near_ref.shape[0]
    for k in range(2):
        mine, rest = slice(k * size, (k + 1) * size), slice((1 - k) * size, (2 - k) * size)

        @pl.when((core == k) & left)
        def _(mine=mine, rest=rest):
            out_ref[...] = product(own_ref[:, mine], near_ref[...]) + product(own_ref[:, rest], far_ref[...])

        @pl.when((core == k) & jnp.logical_not(left))
        def _(mine=mine, rest=rest):
            out_ref[mine, :] = product(near_ref[...], own_ref[...])
            out_ref[rest, :] = product(far_ref[...], own_ref[...])


def level_kernel(bit, own_ref, near_ref, far_ref, out_ref, half_ref):
    combine(bit, 0, own_ref, near_ref, far_ref, out_ref)
    half_of(lax.axis_index("cuts"), out_ref, half_ref)


def last_kernel(own_ref, near_ref, far_ref, block_ref, log_ref, whole_ref):
    combine(0, 1, own_ref, near_ref, far_ref, whole_ref)
    whole = whole_ref[...]
    square = jnp.sum(jnp.sum(whole * whole, axis=0, keepdims=True), axis=1, keepdims=True)
    spread = jnp.sqrt(square / whole.size + 1e-06)
    rows, cols = block_ref.shape
    start = pl.multiple_of(lax.axis_index("tile") * rows, 8)
    core = lax.axis_index("cuts")
    for k in range(whole.shape[1] // cols):

        @pl.when(core == k)
        def _(k=k):
            block_ref[...] = whole_ref[pl.ds(start, rows), k * cols : (k + 1) * cols] / spread

    log_ref[...] = jnp.log(spread)


def plain_leaf(slice_rows, row_owner, leaf_row, exponent, environment, ordering, sign_mask, tiles, cap):
    width = slice_rows.shape[1]
    factor = jnp.where(exponent == -1, 0.5, jnp.where(exponent == 1, 2.0, 1.0)).astype(F32)
    scaled = slice_rows * factor[:, None]
    owners = row_owner[:, 0]
    hits = (owners[:, None] == jnp.arange(tiles, dtype=jnp.int32)[None, :]).astype(jnp.int32)
    position = jnp.sum((jnp.cumsum(hits, axis=0) - hits) * hits, axis=1)
    placed = owners * cap + position
    outgoing = jnp.zeros((tiles * cap, width), F32).at[placed].set(scaled)
    outgoing_rows = jnp.zeros((tiles * cap,), jnp.int32).at[placed].set(leaf_row)
    arrived = lax.all_to_all(outgoing, "tile", split_axis=0, concat_axis=0, tiled=True)
    arrived_rows = lax.all_to_all(outgoing_rows, "tile", split_axis=0, concat_axis=0, tiled=True)
    collected = jnp.zeros((width, width), F32).at[arrived_rows].add(arrived)
    contracted = jnp.dot(collected, environment, precision=lax.Precision.HIGHEST, preferred_element_type=F32)
    columns = jnp.arange(width, dtype=jnp.int32)
    signs = 1.0 - 2.0 * sign_mask[0].astype(F32)
    leaf = contracted + (ordering[0][:, None] == columns[None, :]).astype(F32) * signs[:, None]
    return moved(leaf, routed(0))


def packed_leaf(slice_rows, row_owner, leaf_row, exponent, environment, ordering, sign_mask, tiles, cap):
    count, width = slice_rows.shape
    sets = tiles // 2
    env = moved(environment, routed(0))
    line = lambda a: a.reshape(1, count)
    outgoing = call(
        functools.partial(pack_kernel, tiles, cap),
        [like(2 * cap + PAD, width)] * sets,
        (slice_rows, line(row_owner), line(leaf_row), line(exponent), ordering, sign_mask),
        flops=6 * tiles * cap * count * width,
    )
    near = [None] * sets
    for m in sorted(range(sets), key=lambda m: -m):
        near[m] = moved(outgoing[m], routed(m))
    far = [moved(block, other_core) for block in near]
    (leaf,) = call(
        functools.partial(leaf_kernel, cap, sets),
        [like(width, width)],
        (*near, *far, env),
        flops=10 * width**3,
    )
    return leaf


def body(slice_rows, row_owner, leaf_row, exponent, environment, ordering, sign_mask):
    tiles = lax.axis_size("tile")
    count, width = slice_rows.shape
    cap = max(2, (3 * count + 2 * tiles - 1) // (2 * tiles))
    narrow = cap % 8 == 0 and 2 * cap <= 128 and 2 <= tiles // 2 <= 8 and width % 128 == 0
    make_leaf = packed_leaf if narrow else plain_leaf
    leaf = make_leaf(slice_rows, row_owner, leaf_row, exponent, environment, ordering, sign_mask, tiles, cap)
    whole, half = like(width, width), like(width // 2, width)
    cost = 6 * width**3
    own, part = call(pair_kernel, [whole, half], (leaf, moved(leaf, other_core)), flops=cost)
    for level in range(1, tiles.bit_length() - 1):
        near = moved(part, across(level))
        far = moved(near, other_core)
        own, part = call(functools.partial(level_kernel, level), [whole, half], (own, near, far), flops=cost)
    near = moved(part, across(0))
    far = moved(near, other_core)
    block, log = call(
        last_kernel,
        [like(width // tiles, width // 2), like(1, 1)],
        (own, near, far),
        scratch=[pltpu.VMEM((width, width), F32)],
        flops=cost,
    )
    return block, log.reshape(1)


def solution(mesh):
    return jax.shard_map(
        body,
        mesh=mesh,
        in_specs=(
            P(("groups", "tile", "cuts"), None),
            P(("groups", "tile", "cuts"), None),
            P(("groups", "tile", "cuts")),
            P(("groups", "tile", "cuts")),
            P(("groups", "tile", "cuts"), None),
            P(("groups", "tile", "cuts"), None),
            P(("groups", "tile", "cuts"), None),
        ),
        out_specs=(P(("groups", "tile"), "cuts"), P("groups")),
        check_vma=False,
    )
```

```python
import functools

import jax
import jax.numpy as jnp
from jax import lax
from jax.experimental import pallas as pl
from jax.experimental.pallas import tpu as pltpu
from jax.sharding import PartitionSpec as P

AXES = ("tile", "cuts")
VMEM = pl.BlockSpec(memory_space=pltpu.VMEM)
BF, F32 = jnp.bfloat16, jnp.float32
PAD = 8
GRANT = 16 << 20


def pairs(tiles, place):
    out = []
    for t in range(tiles):
        for c in range(2):
            to, core = place(t, c)
            out.append((t * 2 + c, to * 2 + core))
    return out


def moved(x, place):
    return lax.ppermute(x, AXES, pairs(lax.axis_size("tile"), place))


def routed(m):
    def place(t, c):
        to = t ^ (m << 1)
        return (to ^ 1, c ^ 1) if (t & 1) == c else (to, c)

    return place


def other_core(t, c):
    return t, c ^ 1


def across(level):
    return lambda t, c: (t ^ (1 << level), c)


def mul(a, b, dims=None):
    if dims is None:
        return jnp.dot(a, b, preferred_element_type=F32)
    return lax.dot_general(a, b, (dims, ((), ())), preferred_element_type=F32)


def split2(x):
    hi = x.astype(BF)
    return hi, (x - hi.astype(F32)).astype(BF)


def split3(x):
    hi = x.astype(BF)
    rest = x - hi.astype(F32)
    mid = rest.astype(BF)
    return hi, mid, (rest - mid.astype(F32)).astype(BF)


def product(a, b):
    ah, al = split2(a)
    bh, bl = split2(b)
    return mul(ah, bh) + (mul(ah, bl) + mul(al, bh))


def call(kernel, outs, args, scratch=(), flops=0, held=True, kept=True):
    size = sum(a.size * 4 for a in args) + sum(o.size * 4 for o in outs)
    if held:
        args = [pltpu.with_memory_space_constraint(a, pltpu.VMEM) for a in args]
    return pl.pallas_call(
        kernel,
        out_shape=tuple(pltpu.VMEM(o.shape, o.dtype) if kept else o for o in outs),
        in_specs=[VMEM] * len(args),
        out_specs=tuple([VMEM] * len(outs)),
        scratch_shapes=list(scratch),
        cost_estimate=pl.CostEstimate(flops=flops, bytes_accessed=size, transcendentals=0),
        compiler_params=pltpu.CompilerParams(vmem_limit_bytes=GRANT),
    )(*args)


def like(*shape):
    return jax.ShapeDtypeStruct(shape, F32)


def pack_kernel(tiles, cap, rows_ref, owner_ref, leaf_ref, exp_ref, order_ref, sign_ref, *outs):
    count = rows_ref.shape[0]
    tile = lax.axis_index("tile")
    own = owner_ref[...]
    hits = own == lax.broadcasted_iota(jnp.int32, (tiles, count), 0)
    earlier = lax.broadcasted_iota(jnp.int32, (count, count), 0) < lax.broadcasted_iota(jnp.int32, (count, count), 1)
    before = mul(jnp.where(hits, 1.0, 0.0).astype(BF), jnp.where(earlier, 1.0, 0.0).astype(BF))
    position = jnp.sum(jnp.where(hits, before, 0.0), axis=0, keepdims=True).astype(jnp.int32)
    placed = (own ^ tile) * cap + position
    power = exp_ref[...]
    factor = jnp.where(power == -1, 0.5, jnp.where(power == 1, 2.0, 1.0))
    row = leaf_ref[...] + 1
    which = lax.broadcasted_iota(jnp.int32, (PAD, count), 0)
    digits = jnp.where(which == 0, row >> 4, jnp.where(which == 1, row & 15, 0)).astype(F32).astype(BF)
    hi, mid, lo = split3(rows_ref[...])
    for m, out in enumerate(outs):
        slots = lax.broadcasted_iota(jnp.int32, (2 * cap, count), 0) + m * 2 * cap
        hot = slots == placed
        pick = jnp.where(hot, factor, 0.0).astype(BF)
        out[0 : 2 * cap, :] = mul(pick, hi) + (mul(pick, mid) + mul(pick, lo))
        out[2 * cap : 2 * cap + PAD, :] = jnp.zeros((PAD, out.shape[1]), F32)
        out[2 * cap : 2 * cap + PAD, 0 : 2 * cap] = mul(digits, jnp.where(hot, 1.0, 0.0).astype(BF), ((1,), (1,)))
    signs = 1 - 2 * sign_ref[...]
    outs[0][2 * cap + 2 : 2 * cap + 3, :] = ((order_ref[...] + 1) * signs).astype(F32)


def leaf_kernel(cap, count, *refs):
    near, far, env_ref, leaf_ref = refs[:count], refs[count : 2 * count], refs[2 * count], refs[2 * count + 1]
    width = env_ref.shape[1]
    eh, el = split2(env_ref[...])
    lane = lax.broadcasted_iota(jnp.int32, (1, 128), 1)
    targets = lax.broadcasted_iota(jnp.int32, (width, 128), 0) + 1
    total = None
    for m in range(0, count, 2):
        spread, chosen = [], []
        for i in (m, m + 1):
            block = jnp.concatenate([near[i][0:cap, :], far[i][cap : 2 * cap, :]], axis=0)
            bh, bl = split2(block)
            spread.append(mul(bh, eh) + (mul(bh, el) + mul(bl, eh)))
            spread.append(jnp.zeros((128 - 2 * cap, width), F32))
            digits = jnp.where(lane < cap, near[i][2 * cap : 2 * cap + PAD, 0:128], far[i][2 * cap : 2 * cap + PAD, 0:128])
            to = (digits[0:1, :] * 16.0 + digits[1:2, :]).astype(jnp.int32)
            to = jnp.where(lane < 2 * cap, to, 0)
            chosen.append(jnp.where(targets == to, 1.0, 0.0).astype(BF))
        sh, sl = split2(jnp.concatenate(spread, axis=0))
        pick = jnp.concatenate(chosen, axis=1)
        part = mul(pick, sh) + mul(pick, sl)
        total = part if total is None else total + part
    code = near[0][2 * cap : 2 * cap + PAD, :]
    column = jnp.transpose(code)[:, 2:3]
    bond = (jnp.abs(column) - 1.0).astype(jnp.int32)
    sign = jnp.where(column < 0.0, -1.0, 1.0)
    spots = lax.broadcasted_iota(jnp.int32, (width, width), 1)
    leaf_ref[...] = total + jnp.where(spots == bond, sign, 0.0)


def half_of(core, value, half_ref):
    size = half_ref.shape[0]
    for k in range(2):

        @pl.when(core == k)
        def _(k=k):
            half_ref[...] = value[k * size : (k + 1) * size, :]


def pair_kernel(own_ref, other_ref, out_ref, half_ref):
    core = lax.axis_index("cuts")

    @pl.when(core == 1)
    def _():
        out_ref[...] = product(own_ref[...], other_ref[...])

    @pl.when(core == 0)
    def _():
        out_ref[...] = product(other_ref[...], own_ref[...])

    half_of(core, out_ref, half_ref)


def combine(bit, left_if, own_ref, near_ref, far_ref, out_ref):
    core = lax.axis_index("cuts")
    left = ((lax.axis_index("tile") >> bit) & 1) == left_if
    size = near_ref.shape[0]
    for k in range(2):
        mine, rest = slice(k * size, (k + 1) * size), slice((1 - k) * size, (2 - k) * size)

        @pl.when((core == k) & left)
        def _(mine=mine, rest=rest):
            out_ref[...] = product(own_ref[:, mine], near_ref[...]) + product(own_ref[:, rest], far_ref[...])

        @pl.when((core == k) & jnp.logical_not(left))
        def _(mine=mine, rest=rest):
            out_ref[mine, :] = product(near_ref[...], own_ref[...])
            out_ref[rest, :] = product(far_ref[...], own_ref[...])


def level_kernel(bit, own_ref, near_ref, far_ref, out_ref, half_ref):
    combine(bit, 0, own_ref, near_ref, far_ref, out_ref)
    half_of(lax.axis_index("cuts"), out_ref, half_ref)


def last_kernel(own_ref, near_ref, far_ref, block_ref, log_ref, whole_ref):
    combine(0, 1, own_ref, near_ref, far_ref, whole_ref)
    whole = whole_ref[...]
    square = jnp.sum(jnp.sum(whole * whole, axis=0, keepdims=True), axis=1, keepdims=True)
    spread = jnp.sqrt(square / whole.size + 1e-06)
    rows, cols = block_ref.shape
    start = pl.multiple_of(lax.axis_index("tile") * rows, 8)
    core = lax.axis_index("cuts")
    for k in range(whole.shape[1] // cols):

        @pl.when(core == k)
        def _(k=k):
            block_ref[...] = whole_ref[pl.ds(start, rows), k * cols : (k + 1) * cols] / spread

    log_ref[...] = jnp.log(spread)


def plain_leaf(slice_rows, row_owner, leaf_row, exponent, environment, ordering, sign_mask, tiles, cap):
    width = slice_rows.shape[1]
    factor = jnp.where(exponent == -1, 0.5, jnp.where(exponent == 1, 2.0, 1.0)).astype(F32)
    scaled = slice_rows * factor[:, None]
    owners = row_owner[:, 0]
    hits = (owners[:, None] == jnp.arange(tiles, dtype=jnp.int32)[None, :]).astype(jnp.int32)
    position = jnp.sum((jnp.cumsum(hits, axis=0) - hits) * hits, axis=1)
    placed = owners * cap + position
    outgoing = jnp.zeros((tiles * cap, width), F32).at[placed].set(scaled)
    outgoing_rows = jnp.zeros((tiles * cap,), jnp.int32).at[placed].set(leaf_row)
    arrived = lax.all_to_all(outgoing, "tile", split_axis=0, concat_axis=0, tiled=True)
    arrived_rows = lax.all_to_all(outgoing_rows, "tile", split_axis=0, concat_axis=0, tiled=True)
    collected = jnp.zeros((width, width), F32).at[arrived_rows].add(arrived)
    contracted = jnp.dot(collected, environment, precision=lax.Precision.HIGHEST, preferred_element_type=F32)
    columns = jnp.arange(width, dtype=jnp.int32)
    signs = 1.0 - 2.0 * sign_mask[0].astype(F32)
    leaf = contracted + (ordering[0][:, None] == columns[None, :]).astype(F32) * signs[:, None]
    return moved(leaf, routed(0))


def packed_leaf(slice_rows, row_owner, leaf_row, exponent, environment, ordering, sign_mask, tiles, cap):
    count, width = slice_rows.shape
    sets = tiles // 2
    env = moved(environment, routed(0))
    line = lambda a: a.reshape(1, count)
    outgoing = call(
        functools.partial(pack_kernel, tiles, cap),
        [like(2 * cap + PAD, width)] * sets,
        (slice_rows, line(row_owner), line(leaf_row), line(exponent), ordering, sign_mask),
        flops=6 * tiles * cap * count * width,
        held=False,
    )
    near = [None] * sets
    for m in sorted(range(sets), key=lambda m: -m):
        near[m] = moved(outgoing[m], routed(m))
    far = [moved(block, other_core) for block in near]
    (leaf,) = call(
        functools.partial(leaf_kernel, cap, sets),
        [like(width, width)],
        (*near, *far, env),
        flops=10 * width**3,
    )
    return leaf


def body(slice_rows, row_owner, leaf_row, exponent, environment, ordering, sign_mask):
    tiles = lax.axis_size("tile")
    count, width = slice_rows.shape
    cap = max(2, (3 * count + 2 * tiles - 1) // (2 * tiles))
    narrow = cap % 8 == 0 and 2 * cap <= 128 and 2 <= tiles // 2 <= 8 and width % 128 == 0
    make_leaf = packed_leaf if narrow else plain_leaf
    leaf = make_leaf(slice_rows, row_owner, leaf_row, exponent, environment, ordering, sign_mask, tiles, cap)
    whole, half = like(width, width), like(width // 2, width)
    cost = 6 * width**3
    own, part = call(pair_kernel, [whole, half], (leaf, moved(leaf, other_core)), flops=cost)
    for level in range(1, tiles.bit_length() - 1):
        near = moved(part, across(level))
        far = moved(near, other_core)
        own, part = call(functools.partial(level_kernel, level), [whole, half], (own, near, far), flops=cost)
    near = moved(part, across(0))
    far = moved(near, other_core)
    block, log = call(
        last_kernel,
        [like(width // tiles, width // 2), like(1, 1)],
        (own, near, far),
        scratch=[pltpu.VMEM((width, width), F32)],
        flops=cost,
        kept=False,
    )
    return block, log.reshape(1)


def solution(mesh):
    return jax.shard_map(
        body,
        mesh=mesh,
        in_specs=(
            P(("groups", "tile", "cuts"), None),
            P(("groups", "tile", "cuts"), None),
            P(("groups", "tile", "cuts")),
            P(("groups", "tile", "cuts")),
            P(("groups", "tile", "cuts"), None),
            P(("groups", "tile", "cuts"), None),
            P(("groups", "tile", "cuts"), None),
        ),
        out_specs=(P(("groups", "tile"), "cuts"), P("groups")),
        check_vma=False,
    )
```

```python
import functools

import jax
import jax.numpy as jnp
from jax import lax
from jax.experimental import pallas as pl
from jax.experimental.pallas import tpu as pltpu
from jax.sharding import PartitionSpec as P

AXES = ("tile", "cuts")
VMEM = pl.BlockSpec(memory_space=pltpu.VMEM)
BF, F32 = jnp.bfloat16, jnp.float32
PAD = 8
GRANT = 16 << 20


def pairs(tiles, place):
    out = []
    for t in range(tiles):
        for c in range(2):
            to, core = place(t, c)
            out.append((t * 2 + c, to * 2 + core))
    return out


def moved(x, place):
    return lax.ppermute(x, AXES, pairs(lax.axis_size("tile"), place))


def routed(m):
    def place(t, c):
        to = t ^ (m << 1)
        return (to ^ 1, c ^ 1) if (t & 1) == c else (to, c)

    return place


def other_core(t, c):
    return t, c ^ 1


def across(level):
    return lambda t, c: (t ^ (1 << level), c)


def mul(a, b, dims=None):
    if dims is None:
        return jnp.dot(a, b, preferred_element_type=F32)
    return lax.dot_general(a, b, (dims, ((), ())), preferred_element_type=F32)


def split2(x):
    hi = x.astype(BF)
    return hi, (x - hi.astype(F32)).astype(BF)


def split3(x):
    hi = x.astype(BF)
    rest = x - hi.astype(F32)
    mid = rest.astype(BF)
    return hi, mid, (rest - mid.astype(F32)).astype(BF)


def product(a, b):
    ah, al = split2(a)
    bh, bl = split2(b)
    return mul(ah, bh) + (mul(ah, bl) + mul(al, bh))


def call(kernel, outs, args, scratch=(), flops=0, held=True, kept=True):
    size = sum(a.size * 4 for a in args) + sum(o.size * 4 for o in outs)
    args = [pltpu.with_memory_space_constraint(a, pltpu.VMEM if held else pltpu.HBM) for a in args]
    return pl.pallas_call(
        kernel,
        out_shape=tuple(pltpu.VMEM(o.shape, o.dtype) if kept else o for o in outs),
        in_specs=[VMEM] * len(args),
        out_specs=tuple([VMEM] * len(outs)),
        scratch_shapes=list(scratch),
        cost_estimate=pl.CostEstimate(flops=flops, bytes_accessed=size, transcendentals=0),
        compiler_params=pltpu.CompilerParams(vmem_limit_bytes=GRANT),
    )(*args)


def like(*shape):
    return jax.ShapeDtypeStruct(shape, F32)


def pack_kernel(tiles, cap, rows_ref, owner_ref, leaf_ref, exp_ref, order_ref, sign_ref, *outs):
    count = rows_ref.shape[0]
    tile = lax.axis_index("tile")
    own = owner_ref[...]
    hits = own == lax.broadcasted_iota(jnp.int32, (tiles, count), 0)
    earlier = lax.broadcasted_iota(jnp.int32, (count, count), 0) < lax.broadcasted_iota(jnp.int32, (count, count), 1)
    before = mul(jnp.where(hits, 1.0, 0.0).astype(BF), jnp.where(earlier, 1.0, 0.0).astype(BF))
    position = jnp.sum(jnp.where(hits, before, 0.0), axis=0, keepdims=True).astype(jnp.int32)
    placed = (own ^ tile) * cap + position
    power = exp_ref[...]
    factor = jnp.where(power == -1, 0.5, jnp.where(power == 1, 2.0, 1.0))
    row = leaf_ref[...] + 1
    which = lax.broadcasted_iota(jnp.int32, (PAD, count), 0)
    digits = jnp.where(which == 0, row >> 4, jnp.where(which == 1, row & 15, 0)).astype(F32).astype(BF)
    hi, mid, lo = split3(rows_ref[...])
    for m, out in enumerate(outs):
        slots = lax.broadcasted_iota(jnp.int32, (2 * cap, count), 0) + m * 2 * cap
        hot = slots == placed
        pick = jnp.where(hot, factor, 0.0).astype(BF)
        out[0 : 2 * cap, :] = mul(pick, hi) + (mul(pick, mid) + mul(pick, lo))
        out[2 * cap : 2 * cap + PAD, :] = jnp.zeros((PAD, out.shape[1]), F32)
        out[2 * cap : 2 * cap + PAD, 0 : 2 * cap] = mul(digits, jnp.where(hot, 1.0, 0.0).astype(BF), ((1,), (1,)))
    signs = 1 - 2 * sign_ref[...]
    outs[0][2 * cap + 2 : 2 * cap + 3, :] = ((order_ref[...] + 1) * signs).astype(F32)


def leaf_kernel(cap, count, *refs):
    near, far, env_ref, leaf_ref = refs[:count], refs[count : 2 * count], refs[2 * count], refs[2 * count + 1]
    width = env_ref.shape[1]
    eh, el = split2(env_ref[...])
    lane = lax.broadcasted_iota(jnp.int32, (1, 128), 1)
    targets = lax.broadcasted_iota(jnp.int32, (width, 128), 0) + 1
    total = None
    for m in range(0, count, 2):
        spread, chosen = [], []
        for i in (m, m + 1):
            block = jnp.concatenate([near[i][0:cap, :], far[i][cap : 2 * cap, :]], axis=0)
            bh, bl = split2(block)
            spread.append(mul(bh, eh) + (mul(bh, el) + mul(bl, eh)))
            spread.append(jnp.zeros((128 - 2 * cap, width), F32))
            digits = jnp.where(lane < cap, near[i][2 * cap : 2 * cap + PAD, 0:128], far[i][2 * cap : 2 * cap + PAD, 0:128])
            to = (digits[0:1, :] * 16.0 + digits[1:2, :]).astype(jnp.int32)
            to = jnp.where(lane < 2 * cap, to, 0)
            chosen.append(jnp.where(targets == to, 1.0, 0.0).astype(BF))
        sh, sl = split2(jnp.concatenate(spread, axis=0))
        pick = jnp.concatenate(chosen, axis=1)
        part = mul(pick, sh) + mul(pick, sl)
        total = part if total is None else total + part
    code = near[0][2 * cap : 2 * cap + PAD, :]
    column = jnp.transpose(code)[:, 2:3]
    bond = (jnp.abs(column) - 1.0).astype(jnp.int32)
    sign = jnp.where(column < 0.0, -1.0, 1.0)
    spots = lax.broadcasted_iota(jnp.int32, (width, width), 1)
    leaf_ref[...] = total + jnp.where(spots == bond, sign, 0.0)


def half_of(core, value, half_ref):
    size = half_ref.shape[0]
    for k in range(2):

        @pl.when(core == k)
        def _(k=k):
            half_ref[...] = value[k * size : (k + 1) * size, :]


def pair_kernel(own_ref, other_ref, out_ref, half_ref):
    core = lax.axis_index("cuts")

    @pl.when(core == 1)
    def _():
        out_ref[...] = product(own_ref[...], other_ref[...])

    @pl.when(core == 0)
    def _():
        out_ref[...] = product(other_ref[...], own_ref[...])

    half_of(core, out_ref, half_ref)


def combine(bit, left_if, own_ref, near_ref, far_ref, out_ref):
    core = lax.axis_index("cuts")
    left = ((lax.axis_index("tile") >> bit) & 1) == left_if
    size = near_ref.shape[0]
    for k in range(2):
        mine, rest = slice(k * size, (k + 1) * size), slice((1 - k) * size, (2 - k) * size)

        @pl.when((core == k) & left)
        def _(mine=mine, rest=rest):
            out_ref[...] = product(own_ref[:, mine], near_ref[...]) + product(own_ref[:, rest], far_ref[...])

        @pl.when((core == k) & jnp.logical_not(left))
        def _(mine=mine, rest=rest):
            out_ref[mine, :] = product(near_ref[...], own_ref[...])
            out_ref[rest, :] = product(far_ref[...], own_ref[...])


def level_kernel(bit, own_ref, near_ref, far_ref, out_ref, half_ref):
    combine(bit, 0, own_ref, near_ref, far_ref, out_ref)
    half_of(lax.axis_index("cuts"), out_ref, half_ref)


def last_kernel(own_ref, near_ref, far_ref, block_ref, log_ref, whole_ref):
    combine(0, 1, own_ref, near_ref, far_ref, whole_ref)
    whole = whole_ref[...]
    square = jnp.sum(jnp.sum(whole * whole, axis=0, keepdims=True), axis=1, keepdims=True)
    spread = jnp.sqrt(square / whole.size + 1e-06)
    rows, cols = block_ref.shape
    start = pl.multiple_of(lax.axis_index("tile") * rows, 8)
    core = lax.axis_index("cuts")
    for k in range(whole.shape[1] // cols):

        @pl.when(core == k)
        def _(k=k):
            block_ref[...] = whole_ref[pl.ds(start, rows), k * cols : (k + 1) * cols] / spread

    log_ref[...] = jnp.log(spread)


def product_nt(a, b):
    ah, al = split2(a)
    bh, bl = split2(b)
    last = ((1,), (1,))
    return mul(ah, bh, last) + (mul(ah, bl, last) + mul(al, bh, last))


def fold_pair_kernel(own_ref, other_ref, out_ref, *parts):
    core = lax.axis_index("cuts")
    odd = (lax.axis_index("tile") >> 1) & 1
    for k in range(2):

        @pl.when(core == k)
        def _(k=k):
            left, right = (own_ref, other_ref) if k else (other_ref, own_ref)
            out_ref[...] = product(left[...], right[...])

    @pl.when(odd == 1)
    def _():
        out_ref[...] = jnp.transpose(out_ref[...])

    rows = parts[0].shape[0]
    start = core * (rows * len(parts))
    for p, part in enumerate(parts):
        part[...] = out_ref[pl.ds(pl.multiple_of(start + p * rows, 8), rows), :]


def fold_kernel(near_ref, own_ref, out_ref):
    out_ref[...] = product_nt(near_ref[...], own_ref[...])


def fold_wide_kernel(near_ref, *refs):
    out_ref, pieces = refs[-1], refs[:-1]
    core = lax.axis_index("cuts")
    half = len(pieces) // 2
    size = out_ref.shape[1] // 2
    near = near_ref[...]
    for at, group in ((core, pieces[:half]), (1 - core, pieces[half:])):
        rows = jnp.concatenate([piece[...] for piece in group], axis=0)
        out_ref[:, pl.ds(pl.multiple_of(at * size, 128), size)] = product_nt(near, rows)


def fold_last_kernel(count, *refs):
    own, own_far = refs[:count], refs[count : 2 * count]
    got, got_far = refs[2 * count : 3 * count], refs[3 * count : 4 * count]
    block_ref, send_ref, own_ref, got_ref, whole_ref = refs[4 * count :]
    core, tile = lax.axis_index("cuts"), lax.axis_index("tile")
    side, column, group = (tile >> 2) & 1, tile & 1, tile >> 1
    rows = own[0].shape[0]
    for ref, near, far in ((own_ref, own, own_far), (got_ref, got, got_far)):
        for at, part in ((core, near), (1 - core, far)):
            for p, piece in enumerate(part):
                start = pl.multiple_of(at * (rows * count) + p * rows, 8)
                ref[pl.ds(start, rows), :] = piece[...]

    @pl.when(side == column)
    def _():
        whole_ref[...] = product(own_ref[...], got_ref[...])

    @pl.when(side != column)
    def _():
        whole_ref[...] = product(got_ref[...], own_ref[...])

    whole = whole_ref[...]
    square = jnp.sum(jnp.sum(whole * whole, axis=0, keepdims=True), axis=1, keepdims=True)
    spread = jnp.sqrt(square / whole.size + 1e-06)
    high, cols = block_ref.shape
    for ref, place in ((block_ref, group), (send_ref, group ^ 1)):
        rows_at = pl.multiple_of(place * 2 * high, 128)
        cols_at = pl.multiple_of(core * cols, 128)

        @pl.when(side == 1)
        def _(rows_at=rows_at, cols_at=cols_at):
            got_ref[0 : 2 * high, 0:cols] = whole_ref[pl.ds(rows_at, 2 * high), pl.ds(cols_at, cols)]

        @pl.when(side == 0)
        def _(rows_at=rows_at, cols_at=cols_at):
            got_ref[0 : 2 * high, 0:cols] = jnp.transpose(whole_ref[pl.ds(cols_at, cols), pl.ds(rows_at, 2 * high)])

        ref[0:high, :] = got_ref[pl.ds(pl.multiple_of(column * high, 8), high), 0:cols] / spread
    send_ref[high : high + PAD, :] = jnp.broadcast_to(jnp.log(spread), (PAD, cols))


def plain_leaf(slice_rows, row_owner, leaf_row, exponent, environment, ordering, sign_mask, tiles, cap):
    width = slice_rows.shape[1]
    factor = jnp.where(exponent == -1, 0.5, jnp.where(exponent == 1, 2.0, 1.0)).astype(F32)
    scaled = slice_rows * factor[:, None]
    owners = row_owner[:, 0]
    hits = (owners[:, None] == jnp.arange(tiles, dtype=jnp.int32)[None, :]).astype(jnp.int32)
    position = jnp.sum((jnp.cumsum(hits, axis=0) - hits) * hits, axis=1)
    placed = owners * cap + position
    outgoing = jnp.zeros((tiles * cap, width), F32).at[placed].set(scaled)
    outgoing_rows = jnp.zeros((tiles * cap,), jnp.int32).at[placed].set(leaf_row)
    arrived = lax.all_to_all(outgoing, "tile", split_axis=0, concat_axis=0, tiled=True)
    arrived_rows = lax.all_to_all(outgoing_rows, "tile", split_axis=0, concat_axis=0, tiled=True)
    collected = jnp.zeros((width, width), F32).at[arrived_rows].add(arrived)
    contracted = jnp.dot(collected, environment, precision=lax.Precision.HIGHEST, preferred_element_type=F32)
    columns = jnp.arange(width, dtype=jnp.int32)
    signs = 1.0 - 2.0 * sign_mask[0].astype(F32)
    leaf = contracted + (ordering[0][:, None] == columns[None, :]).astype(F32) * signs[:, None]
    return moved(leaf, routed(0))


def packed_leaf(slice_rows, row_owner, leaf_row, exponent, environment, ordering, sign_mask, tiles, cap):
    count, width = slice_rows.shape
    sets = tiles // 2
    env = moved(environment, routed(0))
    line = lambda a: a.reshape(1, count)
    outgoing = call(
        functools.partial(pack_kernel, tiles, cap),
        [like(2 * cap + PAD, width)] * sets,
        (slice_rows, line(row_owner), line(leaf_row), line(exponent), ordering, sign_mask),
        flops=6 * tiles * cap * count * width,
        held=False,
    )
    near = [None] * sets
    for m in sorted(range(sets), key=lambda m: -m):
        near[m] = moved(outgoing[m], routed(m))
    far = [moved(block, other_core) for block in near]
    (leaf,) = call(
        functools.partial(leaf_kernel, cap, sets),
        [like(width, width)],
        (*near, *far, env),
        flops=10 * width**3,
    )
    return leaf


def body(slice_rows, row_owner, leaf_row, exponent, environment, ordering, sign_mask):
    tiles = lax.axis_size("tile")
    count, width = slice_rows.shape
    cap = max(2, (3 * count + 2 * tiles - 1) // (2 * tiles))
    narrow = cap % 8 == 0 and 2 * cap <= 128 and 2 <= tiles // 2 <= 8 and width % 128 == 0
    make_leaf = packed_leaf if narrow else plain_leaf
    leaf = make_leaf(slice_rows, row_owner, leaf_row, exponent, environment, ordering, sign_mask, tiles, cap)
    if tiles == 8 and width % 512 == 0:
        return center_tree(leaf, tiles, width)
    return plain_tree(leaf, tiles, width)


def center(t, c):
    return (t ^ 6 if t >> 1 in (1, 2) else t), c


def center_tree(leaf, tiles, width):
    count = 2
    rows = width // 2 // count
    cost = 6 * width**2
    whole, piece = like(width, width), like(rows, width)
    own, *parts = call(
        fold_pair_kernel, [whole] + [piece] * count, (leaf, moved(leaf, other_core)), flops=cost * width
    )
    near = [moved(part, across(1)) for part in parts]
    first, first_far, got = [], [], []
    for p in range(count):
        (done,) = call(fold_kernel, [piece], (near[p], own), flops=cost * rows)
        first.append(done)
        got.append(moved(done, center))
        first_far.append(moved(done, other_core))
    mine, mine_far, theirs, theirs_far = [], [], [], []
    for p in range(count):
        (done,) = call(fold_wide_kernel, [piece], (got[p], *first, *first_far), flops=cost * rows)
        mine.append(done)
        theirs.append(moved(done, across(0)))
        mine_far.append(moved(done, other_core))
    theirs_far = [moved(part, other_core) for part in theirs]
    high, cols = width // tiles, width // 2
    block, send = call(
        functools.partial(fold_last_kernel, count),
        [like(high, cols), like(high + PAD, cols)],
        (*mine, *mine_far, *theirs, *theirs_far),
        scratch=[pltpu.VMEM((width, width), F32)] * 3,
        flops=cost * width,
    )
    got = moved(send, across(1))
    group = lax.axis_index("tile") >> 1
    inner = (group == 1) | (group == 2)
    log = jnp.where(inner, send[high, 0], got[high, 0])
    return jnp.where(inner, block, got[:high]), log.reshape(1)


def plain_tree(leaf, tiles, width):
    whole, half = like(width, width), like(width // 2, width)
    cost = 6 * width**3
    own, part = call(pair_kernel, [whole, half], (leaf, moved(leaf, other_core)), flops=cost)
    for level in range(1, tiles.bit_length() - 1):
        near = moved(part, across(level))
        far = moved(near, other_core)
        own, part = call(functools.partial(level_kernel, level), [whole, half], (own, near, far), flops=cost)
    near = moved(part, across(0))
    far = moved(near, other_core)
    block, log = call(
        last_kernel,
        [like(width // tiles, width // 2), like(1, 1)],
        (own, near, far),
        scratch=[pltpu.VMEM((width, width), F32)],
        flops=cost,
        kept=False,
    )
    return block, log.reshape(1)


def solution(mesh):
    return jax.shard_map(
        body,
        mesh=mesh,
        in_specs=(
            P(("groups", "tile", "cuts"), None),
            P(("groups", "tile", "cuts"), None),
            P(("groups", "tile", "cuts")),
            P(("groups", "tile", "cuts")),
            P(("groups", "tile", "cuts"), None),
            P(("groups", "tile", "cuts"), None),
            P(("groups", "tile", "cuts"), None),
        ),
        out_specs=(P(("groups", "tile"), "cuts"), P("groups")),
        check_vma=False,
    )
```

```python
import functools

import jax
import jax.numpy as jnp
from jax import lax
from jax.experimental import pallas as pl
from jax.experimental.pallas import tpu as pltpu
from jax.sharding import PartitionSpec as P


AXES = ("groups", "tile", "cuts")
VMEM = pl.BlockSpec(memory_space=pltpu.VMEM)
BF, F32 = jnp.bfloat16, jnp.float32
PAD = 8
GRANT = 16 << 20


def pairs(groups, tiles, place):
    out = []
    for g in range(groups):
        for t in range(tiles):
            for c in range(2):
                to, core, *cross = place(t, c)
                group = g ^ 1 if cross and (g ^ 1) < groups else g
                out.append(((g * tiles + t) * 2 + c, (group * tiles + to) * 2 + core))
    return out


def moved(x, place):
    return lax.ppermute(x, AXES, pairs(lax.axis_size("groups"), lax.axis_size("tile"), place))


def native():
    return (lax.axis_index("tile") & 1) != lax.axis_index("cuts")


def swapped(t, c):
    return (t ^ 1, c ^ 1) if (t & 1) == c else (t, c, True)


def turned(group, sets):
    return 3 if sets == 4 and group in (1, 2) else 0


def routed(m, sets):
    def place(t, c):
        step = m ^ turned(t >> 1, sets)
        if step == 0:
            return swapped(t, c)
        to = t ^ (step << 1)
        return (to ^ 1, c ^ 1) if (t & 1) == c else (to, c)

    return place


def is_inner(sets):
    group = lax.axis_index("tile") >> 1
    return ((group == 1) | (group == 2)) if sets == 4 else group < 0


def other_core(t, c):
    return t, c ^ 1


def across(level):
    return lambda t, c: (t ^ (1 << level), c)


def mul(a, b, dims=None):
    if dims is None:
        return jnp.dot(a, b, preferred_element_type=F32)
    return lax.dot_general(a, b, (dims, ((), ())), preferred_element_type=F32)


def split2(x):
    hi = x.astype(BF)
    return hi, (x - hi.astype(F32)).astype(BF)


def split3(x):
    hi = x.astype(BF)
    rest = x - hi.astype(F32)
    mid = rest.astype(BF)
    return hi, mid, (rest - mid.astype(F32)).astype(BF)


def product(a, b):
    ah, al = split2(a)
    bh, bl = split2(b)
    return mul(ah, bh) + (mul(ah, bl) + mul(al, bh))


def call(kernel, outs, args, scratch=(), flops=0, held=True, kept=True):
    size = sum(a.size * 4 for a in args) + sum(o.size * 4 for o in outs)
    args = [pltpu.with_memory_space_constraint(a, pltpu.VMEM if held else pltpu.HBM) for a in args]
    return pl.pallas_call(
        kernel,
        out_shape=tuple(pltpu.VMEM(o.shape, o.dtype) if kept else o for o in outs),
        in_specs=[VMEM] * len(args),
        out_specs=tuple([VMEM] * len(outs)),
        scratch_shapes=list(scratch),
        cost_estimate=pl.CostEstimate(flops=flops, bytes_accessed=size, transcendentals=0),
        compiler_params=pltpu.CompilerParams(vmem_limit_bytes=GRANT),
    )(*args)


def like(*shape):
    return jax.ShapeDtypeStruct(shape, F32)


def pack_kernel(tiles, cap, rows_ref, owner_ref, leaf_ref, exp_ref, order_ref, sign_ref, *outs):
    count = rows_ref.shape[0]
    lanes = rows_ref.shape[1] // 128
    last = lanes * 2 * cap
    tile = lax.axis_index("tile")
    own = owner_ref[...]
    hits = own == lax.broadcasted_iota(jnp.int32, (tiles, count), 0)
    earlier = lax.broadcasted_iota(jnp.int32, (count, count), 0) < lax.broadcasted_iota(jnp.int32, (count, count), 1)
    before = mul(jnp.where(hits, 1.0, 0.0).astype(BF), jnp.where(earlier, 1.0, 0.0).astype(BF))
    position = jnp.sum(jnp.where(hits, before, 0.0), axis=0, keepdims=True).astype(jnp.int32)
    flip = jnp.where(is_inner(len(outs)), 6, 0)
    placed = (own ^ tile ^ flip) * cap + position
    power = exp_ref[...]
    factor = jnp.where(power == -1, 0.5, jnp.where(power == 1, 2.0, 1.0))
    row = leaf_ref[...] + 1
    which = lax.broadcasted_iota(jnp.int32, (PAD, count), 0)
    digits = jnp.where(which == 0, row >> 4, jnp.where(which == 1, row & 15, 0)).astype(F32).astype(BF)
    hi, mid, lo = split3(rows_ref[...])
    for m, out in enumerate(outs):
        slots = lax.broadcasted_iota(jnp.int32, (2 * cap, count), 0) + m * 2 * cap
        hot = slots == placed
        pick = jnp.where(hot, factor, 0.0).astype(BF)
        rows = mul(pick, hi) + (mul(pick, mid) + mul(pick, lo))
        for j in range(lanes):
            out[j * 2 * cap : (j + 1) * 2 * cap, :] = rows[:, j * 128 : (j + 1) * 128]
        out[last : last + PAD, :] = jnp.zeros((PAD, 128), F32)
        out[last : last + PAD, 0 : 2 * cap] = mul(digits, jnp.where(hot, 1.0, 0.0).astype(BF), ((1,), (1,)))
    code = ((order_ref[...] + 1) * (1 - 2 * sign_ref[...])).astype(F32)
    for out in (outs[0], outs[-1]):
        for j in range(lanes):
            out[last + 2 + j : last + 3 + j, :] = code[:, j * 128 : (j + 1) * 128]


def spread_rows(cap, blocks, eh, el):
    width = eh.shape[1]
    last = width // 128 * 2 * cap
    lane = lax.broadcasted_iota(jnp.int32, (1, 128), 1)
    targets = lax.broadcasted_iota(jnp.int32, (width, 128), 0) + 1
    spread, chosen = [], []
    for near, far in blocks:
        columns = [
            jnp.concatenate([near[at : at + cap, :], far[at + cap : at + 2 * cap, :]], axis=0)
            for at in range(0, last, 2 * cap)
        ]
        bh, bl = split2(jnp.concatenate(columns, axis=1))
        spread.append(mul(bh, eh) + (mul(bh, el) + mul(bl, eh)))
        spread.append(jnp.zeros((128 - 2 * cap, width), F32))
        digits = jnp.where(lane < cap, near[last : last + PAD, :], far[last : last + PAD, :])
        to = (digits[0:1, :] * 16.0 + digits[1:2, :]).astype(jnp.int32)
        to = jnp.where(lane < 2 * cap, to, 0)
        chosen.append(jnp.where(targets == to, 1.0, 0.0).astype(BF))
    sh, sl = split2(jnp.concatenate(spread, axis=0))
    pick = jnp.concatenate(chosen, axis=1)
    return mul(pick, sh) + mul(pick, sl)


def early_leaf_kernel(cap, sets, *refs):
    env_own_ref, env_got_ref, part_ref, high_ref, low_ref = refs[8:]
    keep, inner = native(), is_inner(sets)
    eh, el = split2(jnp.where(keep, env_own_ref[...], env_got_ref[...]))
    high_ref[...] = eh
    low_ref[...] = el
    blocks = []
    for (own, got, far_own, far_got), stays in ((refs[:4], jnp.logical_not(inner)), (refs[4:8], inner)):
        near = jnp.where(keep & stays, own[...], got[...])
        far = jnp.where(jnp.logical_not(keep) & stays, far_own[...], far_got[...])
        blocks.append((near, far))
    width = eh.shape[1]
    lanes = width // 128
    last = lanes * 2 * cap
    code = jnp.transpose(jnp.where(inner, blocks[1][0][last : last + PAD, :], blocks[0][0][last : last + PAD, :]))
    column = jnp.concatenate([code[:, 2 + j : 3 + j] for j in range(lanes)], axis=0)
    bond = (jnp.abs(column) - 1.0).astype(jnp.int32)
    sign = jnp.where(column < 0.0, -1.0, 1.0)
    spots = lax.broadcasted_iota(jnp.int32, (width, width), 1)
    signed = jnp.where(spots == bond, sign, 0.0)
    part_ref[...] = signed + spread_rows(cap, blocks, eh, el)


def late_leaf_kernel(cap, count, *refs):
    near, far = refs[:count], refs[count : 2 * count]
    high_ref, low_ref, part_ref, leaf_ref = refs[2 * count :]
    leaf_ref[...] = part_ref[...] + spread_rows(cap, list(zip(near, far)), high_ref[...], low_ref[...])


def half_of(core, value, half_ref):
    size = half_ref.shape[0]
    for k in range(2):

        @pl.when(core == k)
        def _(k=k):
            half_ref[...] = value[k * size : (k + 1) * size, :]


def pair_kernel(own_ref, other_ref, out_ref, half_ref):
    core = lax.axis_index("cuts")

    @pl.when(core == 1)
    def _():
        out_ref[...] = product(own_ref[...], other_ref[...])

    @pl.when(core == 0)
    def _():
        out_ref[...] = product(other_ref[...], own_ref[...])

    half_of(core, out_ref, half_ref)


def combine(bit, left_if, own_ref, near_ref, far_ref, out_ref):
    core = lax.axis_index("cuts")
    left = ((lax.axis_index("tile") >> bit) & 1) == left_if
    size = near_ref.shape[0]
    for k in range(2):
        mine, rest = slice(k * size, (k + 1) * size), slice((1 - k) * size, (2 - k) * size)

        @pl.when((core == k) & left)
        def _(mine=mine, rest=rest):
            out_ref[...] = product(own_ref[:, mine], near_ref[...]) + product(own_ref[:, rest], far_ref[...])

        @pl.when((core == k) & jnp.logical_not(left))
        def _(mine=mine, rest=rest):
            out_ref[mine, :] = product(near_ref[...], own_ref[...])
            out_ref[rest, :] = product(far_ref[...], own_ref[...])


def level_kernel(bit, own_ref, near_ref, far_ref, out_ref, half_ref):
    combine(bit, 0, own_ref, near_ref, far_ref, out_ref)
    half_of(lax.axis_index("cuts"), out_ref, half_ref)


def last_kernel(own_ref, near_ref, far_ref, block_ref, log_ref, whole_ref):
    combine(0, 1, own_ref, near_ref, far_ref, whole_ref)
    whole = whole_ref[...]
    square = jnp.sum(jnp.sum(whole * whole, axis=0, keepdims=True), axis=1, keepdims=True)
    spread = jnp.sqrt(square / whole.size + 1e-06)
    rows, cols = block_ref.shape
    start = pl.multiple_of(lax.axis_index("tile") * rows, 8)
    core = lax.axis_index("cuts")
    for k in range(whole.shape[1] // cols):

        @pl.when(core == k)
        def _(k=k):
            block_ref[...] = whole_ref[pl.ds(start, rows), k * cols : (k + 1) * cols] / spread

    log_ref[...] = jnp.log(spread)


def product_nt(a, b):
    ah, al = split2(a)
    bh, bl = split2(b)
    last = ((1,), (1,))
    return mul(ah, bh, last) + (mul(ah, bl, last) + mul(al, bh, last))


def fold_pair_kernel(own_ref, other_ref, out_ref, *parts):
    core = lax.axis_index("cuts")
    odd = (lax.axis_index("tile") >> 1) & 1
    for k in range(2):

        @pl.when(core == k)
        def _(k=k):
            left, right = (own_ref, other_ref) if k else (other_ref, own_ref)
            out_ref[...] = product(left[...], right[...])

    @pl.when(odd == 1)
    def _():
        out_ref[...] = jnp.transpose(out_ref[...])

    start = core * (out_ref.shape[0] // 2)
    for part in parts:
        rows = part.shape[0]
        part[...] = out_ref[pl.ds(pl.multiple_of(start, 8), rows), :]
        start = start + rows


def fold_kernel(near_ref, own_ref, out_ref):
    out_ref[...] = product_nt(near_ref[...], own_ref[...])


def fold_wide_kernel(near_ref, *refs):
    out_ref, pieces = refs[-1], refs[:-1]
    core = lax.axis_index("cuts")
    half = len(pieces) // 2
    size = out_ref.shape[1] // 2
    near = near_ref[...]
    for at, group in ((core, pieces[:half]), (1 - core, pieces[half:])):
        rows = jnp.concatenate([piece[...] for piece in group], axis=0)
        out_ref[:, pl.ds(pl.multiple_of(at * size, 128), size)] = product_nt(near, rows)


def fold_last_kernel(count, *refs):
    own, own_far = refs[:count], refs[count : 2 * count]
    got, got_far = refs[2 * count : 3 * count], refs[3 * count : 4 * count]
    block_ref, send_ref, own_ref, got_ref, whole_ref = refs[4 * count :]
    core, tile = lax.axis_index("cuts"), lax.axis_index("tile")
    side, column, group = (tile >> 2) & 1, tile & 1, tile >> 1
    for ref, near, far in ((own_ref, own, own_far), (got_ref, got, got_far)):
        for at, part in ((core, near), (1 - core, far)):
            start = at * (ref.shape[0] // 2)
            for piece in part:
                rows = piece.shape[0]
                ref[pl.ds(pl.multiple_of(start, 8), rows), :] = piece[...]
                start = start + rows

    @pl.when(side == column)
    def _():
        whole_ref[...] = product(own_ref[...], got_ref[...])

    @pl.when(side != column)
    def _():
        whole_ref[...] = product(got_ref[...], own_ref[...])

    whole = whole_ref[...]
    square = jnp.sum(jnp.sum(whole * whole, axis=0, keepdims=True), axis=1, keepdims=True)
    spread = jnp.sqrt(square / whole.size + 1e-06)
    high, cols = block_ref.shape
    for ref, place in ((block_ref, group), (send_ref, group ^ 1)):
        rows_at = pl.multiple_of(place * 2 * high, 128)
        cols_at = pl.multiple_of(core * cols, 128)

        @pl.when(side == 1)
        def _(rows_at=rows_at, cols_at=cols_at):
            got_ref[0 : 2 * high, 0:cols] = whole_ref[pl.ds(rows_at, 2 * high), pl.ds(cols_at, cols)]

        @pl.when(side == 0)
        def _(rows_at=rows_at, cols_at=cols_at):
            got_ref[0 : 2 * high, 0:cols] = jnp.transpose(whole_ref[pl.ds(cols_at, cols), pl.ds(rows_at, 2 * high)])

        ref[0:high, :] = got_ref[pl.ds(pl.multiple_of(column * high, 8), high), 0:cols] / spread
    send_ref[high : high + PAD, :] = jnp.broadcast_to(jnp.log(spread), (PAD, cols))


def choose_kernel(block_ref, send_ref, got_ref, out_ref, log_ref):
    group = lax.axis_index("tile") >> 1
    inner = (group == 1) | (group == 2)
    high = out_ref.shape[0]
    out_ref[...] = jnp.where(inner, block_ref[...], got_ref[0:high, :])
    log_ref[...] = jnp.where(inner, send_ref[high : high + 1, 0:1], got_ref[high : high + 1, 0:1])


def plain_leaf(slice_rows, row_owner, leaf_row, exponent, environment, ordering, sign_mask, tiles, cap):
    width = slice_rows.shape[1]
    factor = jnp.where(exponent == -1, 0.5, jnp.where(exponent == 1, 2.0, 1.0)).astype(F32)
    scaled = slice_rows * factor[:, None]
    owners = row_owner[:, 0]
    hits = (owners[:, None] == jnp.arange(tiles, dtype=jnp.int32)[None, :]).astype(jnp.int32)
    position = jnp.sum((jnp.cumsum(hits, axis=0) - hits) * hits, axis=1)
    placed = owners * cap + position
    outgoing = jnp.zeros((tiles * cap, width), F32).at[placed].set(scaled)
    outgoing_rows = jnp.zeros((tiles * cap,), jnp.int32).at[placed].set(leaf_row)
    arrived = lax.all_to_all(outgoing, "tile", split_axis=0, concat_axis=0, tiled=True)
    arrived_rows = lax.all_to_all(outgoing_rows, "tile", split_axis=0, concat_axis=0, tiled=True)
    collected = jnp.zeros((width, width), F32).at[arrived_rows].add(arrived)
    contracted = jnp.dot(collected, environment, precision=lax.Precision.HIGHEST, preferred_element_type=F32)
    columns = jnp.arange(width, dtype=jnp.int32)
    signs = 1.0 - 2.0 * sign_mask[0].astype(F32)
    leaf = contracted + (ordering[0][:, None] == columns[None, :]).astype(F32) * signs[:, None]
    return jnp.where(native(), leaf, moved(leaf, swapped))


def packed_leaf(slice_rows, row_owner, leaf_row, exponent, environment, ordering, sign_mask, tiles, cap):
    count, width = slice_rows.shape
    sets = tiles // 2
    env = moved(environment, swapped)
    line = lambda a: a.reshape(1, count)
    outgoing = call(
        functools.partial(pack_kernel, tiles, cap),
        [like(2 * cap * (width // 128) + PAD, 128)] * sets,
        (slice_rows, line(row_owner), line(leaf_row), line(exponent), ordering, sign_mask),
        flops=6 * tiles * cap * count * width,
        held=False,
    )
    near, far = [None] * sets, [None] * sets
    ends = (0, sets - 1)
    for m in (sets - 1, 0, *range(sets - 2, 0, -1)):
        near[m] = moved(outgoing[m], routed(m, sets))
    for m in range(sets):
        far[m] = moved(near[m], other_core)
    far_own = {m: moved(outgoing[m], other_core) for m in ends}
    split = jax.ShapeDtypeStruct((width, width), BF)
    part, high, low = call(
        functools.partial(early_leaf_kernel, cap, sets),
        [like(width, width), split, split],
        [x for m in ends for x in (outgoing[m], near[m], far_own[m], far[m])] + [environment, env],
        flops=5 * width**3,
    )
    if sets == 2:
        return part
    (leaf,) = call(
        functools.partial(late_leaf_kernel, cap, sets - 2),
        [like(width, width)],
        (*near[1:-1], *far[1:-1], high, low, part),
        flops=5 * width**3,
    )
    return leaf


def body(slice_rows, row_owner, leaf_row, exponent, environment, ordering, sign_mask):
    tiles = lax.axis_size("tile")
    count, width = slice_rows.shape
    cap = max(2, (3 * count + 2 * tiles - 1) // (2 * tiles))
    narrow = cap % 8 == 0 and 2 * cap <= 128 and tiles // 2 in (2, 4, 8) and width % 128 == 0 and width <= 768
    make_leaf = packed_leaf if narrow else plain_leaf
    leaf = make_leaf(slice_rows, row_owner, leaf_row, exponent, environment, ordering, sign_mask, tiles, cap)
    if tiles == 8 and width % 512 == 0:
        return center_tree(leaf, tiles, width)
    return plain_tree(leaf, tiles, width)


def center(t, c):
    return (t ^ 6, c) if t >> 1 in (1, 2) else (t, c ^ 1)


def piece_rows(size):
    long = 3 * size // 8
    return long, long, size - 2 * long


def center_tree(leaf, tiles, width):
    sizes = piece_rows(width // 2)
    count = len(sizes)
    cost = 6 * width**2
    pieces = [like(rows, width) for rows in sizes]
    own, *parts = call(
        fold_pair_kernel, [like(width, width)] + pieces, (leaf, moved(leaf, other_core)), flops=cost * width
    )
    near = [moved(part, across(1)) for part in parts]
    first, first_far, got = [], [], []
    for p in range(count):
        (done,) = call(fold_kernel, [pieces[p]], (near[p], own), flops=cost * sizes[p])
        first.append(done)
        got.append(moved(done, center))
        first_far.append(moved(done, other_core))
    mine, mine_far, theirs, theirs_far = [], [], [], []
    for p in range(count):
        (done,) = call(fold_wide_kernel, [pieces[p]], (got[p], *first, *first_far), flops=cost * sizes[p])
        mine.append(done)
        theirs.append(moved(done, across(0)))
        mine_far.append(moved(done, other_core))
    theirs_far = [moved(part, other_core) for part in theirs]
    high, cols = width // tiles, width // 2
    block, send = call(
        functools.partial(fold_last_kernel, count),
        [like(high, cols), like(high + PAD, cols)],
        (*mine, *mine_far, *theirs, *theirs_far),
        scratch=[pltpu.VMEM((width, width), F32)] * 3,
        flops=cost * width,
    )
    out, log = call(
        choose_kernel, [like(high, cols), like(1, 1)], (block, send, moved(send, across(1))), kept=False
    )
    return out, log.reshape(1)


def plain_tree(leaf, tiles, width):
    whole, half = like(width, width), like(width // 2, width)
    cost = 6 * width**3
    own, part = call(pair_kernel, [whole, half], (leaf, moved(leaf, other_core)), flops=cost)
    for level in range(1, tiles.bit_length() - 1):
        near = moved(part, across(level))
        far = moved(near, other_core)
        own, part = call(functools.partial(level_kernel, level), [whole, half], (own, near, far), flops=cost)
    near = moved(part, across(0))
    far = moved(near, other_core)
    block, log = call(
        last_kernel,
        [like(width // tiles, width // 2), like(1, 1)],
        (own, near, far),
        scratch=[pltpu.VMEM((width, width), F32)],
        flops=cost,
        kept=False,
    )
    return block, log.reshape(1)


def solution(mesh):
    return jax.shard_map(
        body,
        mesh=mesh,
        in_specs=(
            P(("groups", "tile", "cuts"), None),
            P(("groups", "tile", "cuts"), None),
            P(("groups", "tile", "cuts")),
            P(("groups", "tile", "cuts")),
            P(("groups", "tile", "cuts"), None),
            P(("groups", "tile", "cuts"), None),
            P(("groups", "tile", "cuts"), None),
        ),
        out_specs=(P(("groups", "tile"), "cuts"), P("groups")),
        check_vma=False,
    )
```

```python
import functools

import jax
import jax.numpy as jnp
from jax import lax
from jax.experimental import pallas as pl
from jax.experimental.pallas import tpu as pltpu
from jax.sharding import PartitionSpec as P


AXES = ("groups", "tile", "cuts")
VMEM = pl.BlockSpec(memory_space=pltpu.VMEM)
BF, F32 = jnp.bfloat16, jnp.float32
PAD = 8
GRANT = 16 << 20


def pairs(groups, tiles, place):
    out = []
    for g in range(groups):
        for t in range(tiles):
            for c in range(2):
                to, core, *cross = place(t, c)
                group = g ^ 1 if cross and (g ^ 1) < groups else g
                out.append(((g * tiles + t) * 2 + c, (group * tiles + to) * 2 + core))
    return out


def moved(x, place):
    return lax.ppermute(x, AXES, pairs(lax.axis_size("groups"), lax.axis_size("tile"), place))


def native():
    return (lax.axis_index("tile") & 1) != lax.axis_index("cuts")


def swapped(t, c):
    return (t ^ 1, c ^ 1) if (t & 1) == c else (t, c, True)


def turned(group, sets):
    return 3 if sets == 4 and group in (1, 2) else 0


def routed(m, sets):
    def place(t, c):
        step = m ^ turned(t >> 1, sets)
        if step == 0:
            return swapped(t, c)
        to = t ^ (step << 1)
        return (to ^ 1, c ^ 1) if (t & 1) == c else (to, c)

    return place


def is_inner(sets):
    group = lax.axis_index("tile") >> 1
    return ((group == 1) | (group == 2)) if sets == 4 else group < 0


def other_core(t, c):
    return t, c ^ 1


def across(level):
    return lambda t, c: (t ^ (1 << level), c)


def mul(a, b, dims=None):
    if dims is None:
        return jnp.dot(a, b, preferred_element_type=F32)
    return lax.dot_general(a, b, (dims, ((), ())), preferred_element_type=F32)


def split2(x):
    hi = x.astype(BF)
    return hi, (x - hi.astype(F32)).astype(BF)


def split3(x):
    hi = x.astype(BF)
    rest = x - hi.astype(F32)
    mid = rest.astype(BF)
    return hi, mid, (rest - mid.astype(F32)).astype(BF)


def product(a, b):
    ah, al = split2(a)
    bh, bl = split2(b)
    return mul(ah, bh) + (mul(ah, bl) + mul(al, bh))


def call(kernel, outs, args, scratch=(), flops=0, held=True, kept=True):
    size = sum(a.size * 4 for a in args) + sum(o.size * 4 for o in outs)
    args = [pltpu.with_memory_space_constraint(a, pltpu.VMEM if held else pltpu.HBM) for a in args]
    return pl.pallas_call(
        kernel,
        out_shape=tuple(pltpu.VMEM(o.shape, o.dtype) if kept else o for o in outs),
        in_specs=[VMEM] * len(args),
        out_specs=tuple([VMEM] * len(outs)),
        scratch_shapes=list(scratch),
        cost_estimate=pl.CostEstimate(flops=flops, bytes_accessed=size, transcendentals=0),
        compiler_params=pltpu.CompilerParams(vmem_limit_bytes=GRANT),
    )(*args)


def like(*shape):
    return jax.ShapeDtypeStruct(shape, F32)


def pack_kernel(tiles, cap, rows_ref, owner_ref, leaf_ref, exp_ref, order_ref, sign_ref, *outs):
    count = rows_ref.shape[0]
    lanes = rows_ref.shape[1] // 128
    last = lanes * 2 * cap
    tile = lax.axis_index("tile")
    own = owner_ref[...]
    hits = own == lax.broadcasted_iota(jnp.int32, (tiles, count), 0)
    earlier = lax.broadcasted_iota(jnp.int32, (count, count), 0) < lax.broadcasted_iota(jnp.int32, (count, count), 1)
    before = mul(jnp.where(hits, 1.0, 0.0).astype(BF), jnp.where(earlier, 1.0, 0.0).astype(BF))
    position = jnp.sum(jnp.where(hits, before, 0.0), axis=0, keepdims=True).astype(jnp.int32)
    flip = jnp.where(is_inner(len(outs)), 6, 0)
    placed = (own ^ tile ^ flip) * cap + position
    power = exp_ref[...]
    factor = jnp.where(power == -1, 0.5, jnp.where(power == 1, 2.0, 1.0))
    row = leaf_ref[...] + 1
    which = lax.broadcasted_iota(jnp.int32, (PAD, count), 0)
    digits = jnp.where(which == 0, row >> 4, jnp.where(which == 1, row & 15, 0)).astype(F32).astype(BF)
    hi, mid, lo = split3(rows_ref[...])
    for m, out in enumerate(outs):
        slots = lax.broadcasted_iota(jnp.int32, (2 * cap, count), 0) + m * 2 * cap
        hot = slots == placed
        pick = jnp.where(hot, factor, 0.0).astype(BF)
        rows = mul(pick, hi) + (mul(pick, mid) + mul(pick, lo))
        for j in range(lanes):
            out[j * 2 * cap : (j + 1) * 2 * cap, :] = rows[:, j * 128 : (j + 1) * 128]
        out[last : last + PAD, :] = jnp.zeros((PAD, 128), F32)
        out[last : last + PAD, 0 : 2 * cap] = mul(digits, jnp.where(hot, 1.0, 0.0).astype(BF), ((1,), (1,)))
    code = ((order_ref[...] + 1) * (1 - 2 * sign_ref[...])).astype(F32)
    for out in (outs[0], outs[-1]):
        for j in range(lanes):
            out[last + 2 + j : last + 3 + j, :] = code[:, j * 128 : (j + 1) * 128]


def spread_rows(cap, blocks, eh, el):
    width = eh.shape[1]
    last = width // 128 * 2 * cap
    lane = lax.broadcasted_iota(jnp.int32, (1, 128), 1)
    targets = lax.broadcasted_iota(jnp.int32, (width, 128), 0) + 1
    spread, chosen = [], []
    for near, far in blocks:
        columns = [
            jnp.concatenate([near[at : at + cap, :], far[at + cap : at + 2 * cap, :]], axis=0)
            for at in range(0, last, 2 * cap)
        ]
        bh, bl = split2(jnp.concatenate(columns, axis=1))
        spread.append(mul(bh, eh) + (mul(bh, el) + mul(bl, eh)))
        spread.append(jnp.zeros((128 - 2 * cap, width), F32))
        digits = jnp.where(lane < cap, near[last : last + PAD, :], far[last : last + PAD, :])
        to = (digits[0:1, :] * 16.0 + digits[1:2, :]).astype(jnp.int32)
        to = jnp.where(lane < 2 * cap, to, 0)
        chosen.append(jnp.where(targets == to, 1.0, 0.0).astype(BF))
    sh, sl = split2(jnp.concatenate(spread, axis=0))
    pick = jnp.concatenate(chosen, axis=1)
    return mul(pick, sh) + mul(pick, sl)


def early_leaf_kernel(cap, sets, *refs):
    env_own_ref, env_got_ref, part_ref, high_ref, low_ref = refs[8:]
    keep, inner = native(), is_inner(sets)
    eh, el = split2(jnp.where(keep, env_own_ref[...], env_got_ref[...]))
    high_ref[...] = eh
    low_ref[...] = el
    blocks = []
    for (own, got, far_own, far_got), stays in ((refs[:4], jnp.logical_not(inner)), (refs[4:8], inner)):
        near = jnp.where(keep & stays, own[...], got[...])
        far = jnp.where(jnp.logical_not(keep) & stays, far_own[...], far_got[...])
        blocks.append((near, far))
    width = eh.shape[1]
    lanes = width // 128
    last = lanes * 2 * cap
    code = jnp.transpose(jnp.where(inner, blocks[1][0][last : last + PAD, :], blocks[0][0][last : last + PAD, :]))
    column = jnp.concatenate([code[:, 2 + j : 3 + j] for j in range(lanes)], axis=0)
    bond = (jnp.abs(column) - 1.0).astype(jnp.int32)
    sign = jnp.where(column < 0.0, -1.0, 1.0)
    spots = lax.broadcasted_iota(jnp.int32, (width, width), 1)
    signed = jnp.where(spots == bond, sign, 0.0)
    part_ref[...] = signed + spread_rows(cap, blocks, eh, el)


def late_leaf_kernel(cap, count, *refs):
    near, far = refs[:count], refs[count : 2 * count]
    high_ref, low_ref, part_ref, leaf_ref = refs[2 * count :]
    leaf_ref[...] = part_ref[...] + spread_rows(cap, list(zip(near, far)), high_ref[...], low_ref[...])


def half_of(core, value, half_ref):
    size = half_ref.shape[0]
    for k in range(2):

        @pl.when(core == k)
        def _(k=k):
            half_ref[...] = value[k * size : (k + 1) * size, :]


def pair_kernel(own_ref, other_ref, out_ref, half_ref):
    core = lax.axis_index("cuts")

    @pl.when(core == 1)
    def _():
        out_ref[...] = product(own_ref[...], other_ref[...])

    @pl.when(core == 0)
    def _():
        out_ref[...] = product(other_ref[...], own_ref[...])

    half_of(core, out_ref, half_ref)


def combine(bit, left_if, own_ref, near_ref, far_ref, out_ref):
    core = lax.axis_index("cuts")
    left = ((lax.axis_index("tile") >> bit) & 1) == left_if
    size = near_ref.shape[0]
    for k in range(2):
        mine, rest = slice(k * size, (k + 1) * size), slice((1 - k) * size, (2 - k) * size)

        @pl.when((core == k) & left)
        def _(mine=mine, rest=rest):
            out_ref[...] = product(own_ref[:, mine], near_ref[...]) + product(own_ref[:, rest], far_ref[...])

        @pl.when((core == k) & jnp.logical_not(left))
        def _(mine=mine, rest=rest):
            out_ref[mine, :] = product(near_ref[...], own_ref[...])
            out_ref[rest, :] = product(far_ref[...], own_ref[...])


def level_kernel(bit, own_ref, near_ref, far_ref, out_ref, half_ref):
    combine(bit, 0, own_ref, near_ref, far_ref, out_ref)
    half_of(lax.axis_index("cuts"), out_ref, half_ref)


def last_kernel(own_ref, near_ref, far_ref, block_ref, log_ref, whole_ref):
    combine(0, 1, own_ref, near_ref, far_ref, whole_ref)
    whole = whole_ref[...]
    square = jnp.sum(jnp.sum(whole * whole, axis=0, keepdims=True), axis=1, keepdims=True)
    spread = jnp.sqrt(square / whole.size + 1e-06)
    rows, cols = block_ref.shape
    start = pl.multiple_of(lax.axis_index("tile") * rows, 8)
    core = lax.axis_index("cuts")
    for k in range(whole.shape[1] // cols):

        @pl.when(core == k)
        def _(k=k):
            block_ref[...] = whole_ref[pl.ds(start, rows), k * cols : (k + 1) * cols] / spread

    log_ref[...] = jnp.log(spread)


def product_nt(a, b):
    ah, al = split2(a)
    bh, bl = split2(b)
    last = ((1,), (1,))
    return mul(ah, bh, last) + (mul(ah, bl, last) + mul(al, bh, last))


def fold_half(flip, own_ref, other_ref, half_ref):
    core = lax.axis_index("cuts")
    side = (lax.axis_index("tile") >> 2) & 1
    size = half_ref.shape[0]
    for k in range(2):
        left, right = (own_ref, other_ref) if k else (other_ref, own_ref)
        at = slice((k ^ flip) * size, ((k ^ flip) + 1) * size)

        @pl.when((core == k) & (side == 0))
        def _(left=left, right=right, at=at):
            half_ref[...] = product(left[at, :], right[...])

        @pl.when((core == k) & (side == 1))
        def _(left=left, right=right, at=at):
            half_ref[...] = jnp.transpose(product(left[...], right[:, at]))


def fold_own_kernel(own_ref, other_ref, high_ref, low_ref, *refs):
    half_ref, parts = refs[-1], refs[:-1]
    fold_half(0, own_ref, other_ref, half_ref)
    start = 0
    for part in parts:
        part[...] = half_ref[start : start + part.shape[0], :]
        start += part.shape[0]
    high_ref[...], low_ref[...] = split2(half_ref[...])


def fold_rest_kernel(own_ref, other_ref, high_ref, low_ref, half_ref):
    fold_half(1, own_ref, other_ref, half_ref)
    high_ref[...], low_ref[...] = split2(half_ref[...])


def fold_kernel(near_ref, high_ref, low_ref, rest_high_ref, rest_low_ref, out_ref):
    core = lax.axis_index("cuts")
    size = high_ref.shape[0]
    total = None
    for at, high, low in ((core, high_ref, low_ref), (1 - core, rest_high_ref, rest_low_ref)):
        ah, al = split2(near_ref[:, pl.ds(pl.multiple_of(at * size, 128), size)])
        part = mul(ah, high[...]) + (mul(ah, low[...]) + mul(al, high[...]))
        total = part if total is None else total + part
    out_ref[...] = total


def fold_wide_kernel(*refs):
    out_ref, groups = refs[-1], refs[0]
    at, used = 0, 1
    for count in groups:
        near, pieces = refs[used][...], refs[used + 1 : used + 1 + count]
        rows = jnp.concatenate([piece[...] for piece in pieces], axis=0)
        out_ref[:, at : at + rows.shape[0]] = product_nt(near, rows)
        at += rows.shape[0]
        used += 1 + count


def gather_pieces(mine, ref, pieces):
    first, second, third = pieces
    size = ref.shape[0] // 2
    long = first.shape[0]
    body = 2 * long
    tail = size - body
    own, other = mine * size, (1 - mine) * size
    at = own
    for piece, low, high in ((first, second, 4 * long + 2 * tail), (second, second, 4 * long), (third, third, 4 * long)):
        rows = slice(at, at + piece.shape[0])
        ref[rows, own : own + body] = piece[:, 0:body]
        ref[rows, other : other + body] = piece[:, body : 2 * body]
        ref[rows, own + body : own + size] = low[:, high : high + tail]
        ref[rows, other + body : other + size] = low[:, high + tail : high + 2 * tail]
        at += piece.shape[0]


def gather_both(near, far, ref):
    core = lax.axis_index("cuts")
    for k in range(2):

        @pl.when(core == k)
        def _(k=k):
            gather_pieces(k, ref, near)
            gather_pieces(1 - k, ref, far)


def fold_ready_kernel(count, *refs):
    near, far, (high_ref, low_ref, own_ref) = refs[:count], refs[count : 2 * count], refs[2 * count :]
    gather_both(near, far, own_ref)
    high_ref[...], low_ref[...] = split2(own_ref[...])


def fold_last_kernel(count, *refs):
    high_ref, low_ref, *refs = refs
    block_ref, send_ref, got_ref, whole_ref = refs[2 * count :]
    gather_both(refs[:count], refs[count : 2 * count], got_ref)
    core, tile = lax.axis_index("cuts"), lax.axis_index("tile")
    side, column, group = (tile >> 2) & 1, tile & 1, tile >> 1

    @pl.when(side == column)
    def _():
        gh, gl = split2(got_ref[...])
        whole_ref[...] = mul(high_ref[...], gh) + (mul(high_ref[...], gl) + mul(low_ref[...], gh))

    @pl.when(side != column)
    def _():
        gh, gl = split2(got_ref[...])
        whole_ref[...] = mul(gh, high_ref[...]) + (mul(gl, high_ref[...]) + mul(gh, low_ref[...]))

    whole = whole_ref[...]
    square = jnp.sum(jnp.sum(whole * whole, axis=0, keepdims=True), axis=1, keepdims=True)
    spread = jnp.sqrt(square / whole.size + 1e-06)
    high, cols = block_ref.shape
    for ref, place in ((block_ref, group), (send_ref, group ^ 1)):
        rows_at = pl.multiple_of(place * 2 * high, 128)
        cols_at = pl.multiple_of(core * cols, 128)

        @pl.when(side == 1)
        def _(rows_at=rows_at, cols_at=cols_at):
            got_ref[0 : 2 * high, 0:cols] = whole_ref[pl.ds(rows_at, 2 * high), pl.ds(cols_at, cols)]

        @pl.when(side == 0)
        def _(rows_at=rows_at, cols_at=cols_at):
            got_ref[0 : 2 * high, 0:cols] = jnp.transpose(whole_ref[pl.ds(cols_at, cols), pl.ds(rows_at, 2 * high)])

        ref[0:high, :] = got_ref[pl.ds(pl.multiple_of(column * high, 8), high), 0:cols] / spread
    send_ref[high : high + PAD, :] = jnp.broadcast_to(jnp.log(spread), (PAD, cols))


def choose_kernel(block_ref, send_ref, got_ref, out_ref, log_ref):
    group = lax.axis_index("tile") >> 1
    inner = (group == 1) | (group == 2)
    high = out_ref.shape[0]
    out_ref[...] = jnp.where(inner, block_ref[...], got_ref[0:high, :])
    log_ref[...] = jnp.where(inner, send_ref[high : high + 1, 0:1], got_ref[high : high + 1, 0:1])


def plain_leaf(slice_rows, row_owner, leaf_row, exponent, environment, ordering, sign_mask, tiles, cap):
    width = slice_rows.shape[1]
    factor = jnp.where(exponent == -1, 0.5, jnp.where(exponent == 1, 2.0, 1.0)).astype(F32)
    scaled = slice_rows * factor[:, None]
    owners = row_owner[:, 0]
    hits = (owners[:, None] == jnp.arange(tiles, dtype=jnp.int32)[None, :]).astype(jnp.int32)
    position = jnp.sum((jnp.cumsum(hits, axis=0) - hits) * hits, axis=1)
    placed = owners * cap + position
    outgoing = jnp.zeros((tiles * cap, width), F32).at[placed].set(scaled)
    outgoing_rows = jnp.zeros((tiles * cap,), jnp.int32).at[placed].set(leaf_row)
    arrived = lax.all_to_all(outgoing, "tile", split_axis=0, concat_axis=0, tiled=True)
    arrived_rows = lax.all_to_all(outgoing_rows, "tile", split_axis=0, concat_axis=0, tiled=True)
    collected = jnp.zeros((width, width), F32).at[arrived_rows].add(arrived)
    contracted = jnp.dot(collected, environment, precision=lax.Precision.HIGHEST, preferred_element_type=F32)
    columns = jnp.arange(width, dtype=jnp.int32)
    signs = 1.0 - 2.0 * sign_mask[0].astype(F32)
    leaf = contracted + (ordering[0][:, None] == columns[None, :]).astype(F32) * signs[:, None]
    return jnp.where(native(), leaf, moved(leaf, swapped))


def packed_leaf(slice_rows, row_owner, leaf_row, exponent, environment, ordering, sign_mask, tiles, cap):
    count, width = slice_rows.shape
    sets = tiles // 2
    env = moved(environment, swapped)
    line = lambda a: a.reshape(1, count)
    outgoing = call(
        functools.partial(pack_kernel, tiles, cap),
        [like(2 * cap * (width // 128) + PAD, 128)] * sets,
        (slice_rows, line(row_owner), line(leaf_row), line(exponent), ordering, sign_mask),
        flops=6 * tiles * cap * count * width,
        held=False,
    )
    near, far = [None] * sets, [None] * sets
    ends = (0, sets - 1)
    for m in (sets - 1, 0, *range(sets - 2, 0, -1)):
        near[m] = moved(outgoing[m], routed(m, sets))
    for m in range(sets):
        far[m] = moved(near[m], other_core)
    far_own = {m: moved(outgoing[m], other_core) for m in ends}
    split = jax.ShapeDtypeStruct((width, width), BF)
    part, high, low = call(
        functools.partial(early_leaf_kernel, cap, sets),
        [like(width, width), split, split],
        [x for m in ends for x in (outgoing[m], near[m], far_own[m], far[m])] + [environment, env],
        flops=5 * width**3,
    )
    if sets == 2:
        return part
    (leaf,) = call(
        functools.partial(late_leaf_kernel, cap, sets - 2),
        [like(width, width)],
        (*near[1:-1], *far[1:-1], high, low, part),
        flops=5 * width**3,
    )
    return leaf


def body(slice_rows, row_owner, leaf_row, exponent, environment, ordering, sign_mask):
    tiles = lax.axis_size("tile")
    count, width = slice_rows.shape
    cap = max(2, (3 * count + 2 * tiles - 1) // (2 * tiles))
    narrow = cap % 8 == 0 and 2 * cap <= 128 and tiles // 2 in (2, 4, 8) and width % 128 == 0 and width <= 768
    make_leaf = packed_leaf if narrow else plain_leaf
    leaf = make_leaf(slice_rows, row_owner, leaf_row, exponent, environment, ordering, sign_mask, tiles, cap)
    if tiles == 8 and width % 512 == 0:
        return center_tree(leaf, tiles, width)
    return plain_tree(leaf, tiles, width)


def center(t, c):
    return (t ^ 6, c) if t >> 1 in (1, 2) else (t, c ^ 1)


def piece_rows(size):
    long = 3 * size // 8
    return long, long, size - 2 * long


def center_tree(leaf, tiles, width):
    sizes = piece_rows(width // 2)
    count = len(sizes)
    cost = 6 * width**2
    pieces = [like(rows, width) for rows in sizes]
    half = jax.ShapeDtypeStruct((width // 2, width), BF)
    scratch = [pltpu.VMEM((width // 2, width), F32)]
    other = moved(leaf, other_core)
    high, low, *parts = call(
        fold_own_kernel, [half, half] + pieces, (leaf, other), scratch=scratch, flops=cost * width // 2
    )
    rest = call(fold_rest_kernel, [half, half], (leaf, other), scratch=scratch, flops=cost * width // 2)
    near = [moved(part, across(1)) for part in parts]
    first, first_far, got = [], [], []
    for p in range(count):
        (done,) = call(fold_kernel, [pieces[p]], (near[p], high, low, *rest), flops=cost * sizes[p])
        first.append(done)
        got.append(moved(done, center))
        first_far.append(moved(done, other_core))
    mine, mine_far, theirs = [], [], []
    long, last = first[:2] + first_far[:2], [first[2], first_far[2]]
    for p, groups in enumerate(([(0, long)], [(1, long + last), (0, last)], [(2, long + last)])):
        columns = [sum(piece.shape[0] for piece in pieces_in) for _, pieces_in in groups]
        args = [x for q, pieces_in in groups for x in (got[q], *pieces_in)]
        kernel = functools.partial(fold_wide_kernel, [len(pieces_in) for _, pieces_in in groups])
        (done,) = call(kernel, [like(sizes[p], sum(columns))], args, flops=6 * width * sizes[p] * sum(columns))
        mine.append(done)
        theirs.append(moved(done, across(0)))
        mine_far.append(moved(done, other_core))
    theirs_far = [moved(part, other_core) for part in theirs]
    tall, cols = width // tiles, width // 2
    split = jax.ShapeDtypeStruct((width, width), BF)
    own = call(
        functools.partial(fold_ready_kernel, count),
        [split, split],
        (*mine, *mine_far),
        scratch=[pltpu.VMEM((width, width), F32)],
        flops=width * width,
    )
    block, send = call(
        functools.partial(fold_last_kernel, count),
        [like(tall, cols), like(tall + PAD, cols)],
        (*own, *theirs, *theirs_far),
        scratch=[pltpu.VMEM((width, width), F32)] * 2,
        flops=cost * width,
    )
    out, log = call(
        choose_kernel, [like(tall, cols), like(1, 1)], (block, send, moved(send, across(1))), kept=False
    )
    return out, log.reshape(1)


def plain_tree(leaf, tiles, width):
    whole, half = like(width, width), like(width // 2, width)
    cost = 6 * width**3
    own, part = call(pair_kernel, [whole, half], (leaf, moved(leaf, other_core)), flops=cost)
    for level in range(1, tiles.bit_length() - 1):
        near = moved(part, across(level))
        far = moved(near, other_core)
        own, part = call(functools.partial(level_kernel, level), [whole, half], (own, near, far), flops=cost)
    near = moved(part, across(0))
    far = moved(near, other_core)
    block, log = call(
        last_kernel,
        [like(width // tiles, width // 2), like(1, 1)],
        (own, near, far),
        scratch=[pltpu.VMEM((width, width), F32)],
        flops=cost,
        kept=False,
    )
    return block, log.reshape(1)


def solution(mesh):
    return jax.shard_map(
        body,
        mesh=mesh,
        in_specs=(
            P(("groups", "tile", "cuts"), None),
            P(("groups", "tile", "cuts"), None),
            P(("groups", "tile", "cuts")),
            P(("groups", "tile", "cuts")),
            P(("groups", "tile", "cuts"), None),
            P(("groups", "tile", "cuts"), None),
            P(("groups", "tile", "cuts"), None),
        ),
        out_specs=(P(("groups", "tile"), "cuts"), P("groups")),
        check_vma=False,
    )
```

```python
import functools

import jax
import jax.numpy as jnp
from jax import lax
from jax.experimental import pallas as pl
from jax.experimental.pallas import tpu as pltpu
from jax.sharding import PartitionSpec as P


AXES = ("groups", "tile", "cuts")
VMEM = pl.BlockSpec(memory_space=pltpu.VMEM)
BF, F32 = jnp.bfloat16, jnp.float32
PAD = 8
GRANT = 16 << 20


def pairs(groups, tiles, place):
    out = []
    for g in range(groups):
        for t in range(tiles):
            for c in range(2):
                to, core, *cross = place(t, c)
                group = g ^ 1 if cross and (g ^ 1) < groups else g
                out.append(((g * tiles + t) * 2 + c, (group * tiles + to) * 2 + core))
    return out


def moved(x, place):
    return lax.ppermute(x, AXES, pairs(lax.axis_size("groups"), lax.axis_size("tile"), place))


def native():
    return (lax.axis_index("tile") & 1) != lax.axis_index("cuts")


def swapped(t, c):
    return (t ^ 1, c ^ 1) if (t & 1) == c else (t, c, True)


def turned(group, sets):
    return 3 if sets == 4 and group in (1, 2) else 0


def routed(m, sets):
    def place(t, c):
        step = m ^ turned(t >> 1, sets)
        if step == 0:
            return swapped(t, c)
        to = t ^ (step << 1)
        return (to ^ 1, c ^ 1) if (t & 1) == c else (to, c)

    return place


def is_inner(sets):
    group = lax.axis_index("tile") >> 1
    return ((group == 1) | (group == 2)) if sets == 4 else group < 0


def other_core(t, c):
    return t, c ^ 1


def across(level):
    return lambda t, c: (t ^ (1 << level), c)


def mul(a, b, dims=None):
    if dims is None:
        return jnp.dot(a, b, preferred_element_type=F32)
    return lax.dot_general(a, b, (dims, ((), ())), preferred_element_type=F32)


def split2(x):
    hi = x.astype(BF)
    return hi, (x - hi.astype(F32)).astype(BF)


def split3(x):
    hi = x.astype(BF)
    rest = x - hi.astype(F32)
    mid = rest.astype(BF)
    return hi, mid, (rest - mid.astype(F32)).astype(BF)


def product(a, b):
    ah, al = split2(a)
    bh, bl = split2(b)
    return mul(ah, bh) + (mul(ah, bl) + mul(al, bh))


def call(kernel, outs, args, scratch=(), flops=0, held=True, kept=True):
    size = sum(a.size * 4 for a in args) + sum(o.size * 4 for o in outs)
    args = [pltpu.with_memory_space_constraint(a, pltpu.VMEM if held else pltpu.HBM) for a in args]
    return pl.pallas_call(
        kernel,
        out_shape=tuple(pltpu.VMEM(o.shape, o.dtype) if kept else o for o in outs),
        in_specs=[VMEM] * len(args),
        out_specs=tuple([VMEM] * len(outs)),
        scratch_shapes=list(scratch),
        cost_estimate=pl.CostEstimate(flops=flops, bytes_accessed=size, transcendentals=0),
        compiler_params=pltpu.CompilerParams(vmem_limit_bytes=GRANT),
    )(*args)


def like(*shape):
    return jax.ShapeDtypeStruct(shape, F32)


def pack_kernel(tiles, cap, rows_ref, owner_ref, leaf_ref, exp_ref, order_ref, sign_ref, *outs):
    count = rows_ref.shape[0]
    lanes = rows_ref.shape[1] // 128
    last = lanes * 2 * cap
    tile = lax.axis_index("tile")
    own = owner_ref[...]
    hits = own == lax.broadcasted_iota(jnp.int32, (tiles, count), 0)
    earlier = lax.broadcasted_iota(jnp.int32, (count, count), 0) < lax.broadcasted_iota(jnp.int32, (count, count), 1)
    before = mul(jnp.where(hits, 1.0, 0.0).astype(BF), jnp.where(earlier, 1.0, 0.0).astype(BF))
    position = jnp.sum(jnp.where(hits, before, 0.0), axis=0, keepdims=True).astype(jnp.int32)
    flip = jnp.where(is_inner(len(outs)), 6, 0)
    placed = (own ^ tile ^ flip) * cap + position
    power = exp_ref[...]
    factor = jnp.where(power == -1, 0.5, jnp.where(power == 1, 2.0, 1.0))
    row = leaf_ref[...] + 1
    which = lax.broadcasted_iota(jnp.int32, (PAD, count), 0)
    digits = jnp.where(which == 0, row >> 4, jnp.where(which == 1, row & 15, 0)).astype(F32).astype(BF)
    hi, mid, lo = split3(rows_ref[...])
    for m, out in enumerate(outs):
        slots = lax.broadcasted_iota(jnp.int32, (2 * cap, count), 0) + m * 2 * cap
        hot = slots == placed
        pick = jnp.where(hot, factor, 0.0).astype(BF)
        rows = mul(pick, hi) + (mul(pick, mid) + mul(pick, lo))
        for j in range(lanes):
            out[j * 2 * cap : (j + 1) * 2 * cap, :] = rows[:, j * 128 : (j + 1) * 128]
        out[last : last + PAD, :] = jnp.zeros((PAD, 128), F32)
        out[last : last + PAD, 0 : 2 * cap] = mul(digits, jnp.where(hot, 1.0, 0.0).astype(BF), ((1,), (1,)))
    code = ((order_ref[...] + 1) * (1 - 2 * sign_ref[...])).astype(F32)
    for out in (outs[0], outs[-1]):
        for j in range(lanes):
            out[last + 2 + j : last + 3 + j, :] = code[:, j * 128 : (j + 1) * 128]


def spread_rows(cap, half, blocks, eh, el):
    width = eh.shape[1]
    last = width // 128 * 2 * cap
    lane = lax.broadcasted_iota(jnp.int32, (1, 128), 1)
    targets = lax.broadcasted_iota(jnp.int32, (width, 128), 0) + 1
    gap = jnp.zeros((64 - cap, width), F32)
    rows, chosen = [], []
    for first, second in zip(blocks[::2], blocks[1::2]):
        for block in (first, second):
            columns = [block[at + half * cap : at + (half + 1) * cap, :] for at in range(0, last, 2 * cap)]
            rows += [jnp.concatenate(columns, axis=1), gap]
        ends = [block[last : last + PAD, :] for block in (first, second)]
        to = [(end[0:1, :] * 16.0 + end[1:2, :]).astype(jnp.int32) for end in ends]
        at = [pltpu.roll(jnp.broadcast_to(t, (PAD, 128)), (j * 64 - half * cap) % 128, 1)[0:1, :] for j, t in enumerate(to)]
        both = jnp.where(lane < 64, jnp.where(lane < cap, at[0], 0), jnp.where(lane < 64 + cap, at[1], 0))
        chosen.append(jnp.where(targets == both, 1.0, 0.0).astype(BF))
    rh, rl = split2(jnp.concatenate(rows, axis=0))
    sh, sl = split2(mul(rh, eh) + (mul(rh, el) + mul(rl, eh)))
    pick = jnp.concatenate(chosen, axis=1)
    return mul(pick, sh) + mul(pick, sl)


def early_leaf_kernel(cap, sets, *refs):
    packed_first, packed_last, env_own_ref, env_got_ref, *refs = refs
    near, (part_ref, high_ref, low_ref) = refs[:sets], refs[sets:]
    keep, inner = native(), is_inner(sets)
    eh, el = split2(jnp.where(keep, env_own_ref[...], env_got_ref[...]))
    high_ref[...] = eh
    low_ref[...] = el
    blocks = [ref[...] for ref in near]
    blocks[0] = jnp.where(keep & jnp.logical_not(inner), packed_first[...], blocks[0])
    blocks[-1] = jnp.where(keep & inner, packed_last[...], blocks[-1])
    width = eh.shape[1]
    lanes = width // 128
    last = lanes * 2 * cap
    code = jnp.transpose(jnp.where(inner, blocks[-1][last : last + PAD, :], blocks[0][last : last + PAD, :]))
    column = jnp.concatenate([code[:, 2 + j : 3 + j] for j in range(lanes)], axis=0)
    bond = (jnp.abs(column) - 1.0).astype(jnp.int32)
    sign = jnp.where(column < 0.0, -1.0, 1.0)
    spots = lax.broadcasted_iota(jnp.int32, (width, width), 1)
    signed = jnp.where(spots == bond, sign, 0.0)
    part_ref[...] = signed + spread_rows(cap, 0, blocks, eh, el)


def late_leaf_kernel(cap, sets, *refs):
    packed_first, packed_last, high_ref, low_ref, part_ref, *refs = refs
    far, leaf_ref = refs[:sets], refs[sets]
    drop, inner = jnp.logical_not(native()), is_inner(sets)
    blocks = [ref[...] for ref in far]
    blocks[0] = jnp.where(drop & jnp.logical_not(inner), packed_first[...], blocks[0])
    blocks[-1] = jnp.where(drop & inner, packed_last[...], blocks[-1])
    leaf_ref[...] = part_ref[...] + spread_rows(cap, 1, blocks, high_ref[...], low_ref[...])


def half_of(core, value, half_ref):
    size = half_ref.shape[0]
    for k in range(2):

        @pl.when(core == k)
        def _(k=k):
            half_ref[...] = value[k * size : (k + 1) * size, :]


def pair_kernel(own_ref, other_ref, out_ref, half_ref):
    core = lax.axis_index("cuts")

    @pl.when(core == 1)
    def _():
        out_ref[...] = product(own_ref[...], other_ref[...])

    @pl.when(core == 0)
    def _():
        out_ref[...] = product(other_ref[...], own_ref[...])

    half_of(core, out_ref, half_ref)


def combine(bit, left_if, own_ref, near_ref, far_ref, out_ref):
    core = lax.axis_index("cuts")
    left = ((lax.axis_index("tile") >> bit) & 1) == left_if
    size = near_ref.shape[0]
    for k in range(2):
        mine, rest = slice(k * size, (k + 1) * size), slice((1 - k) * size, (2 - k) * size)

        @pl.when((core == k) & left)
        def _(mine=mine, rest=rest):
            out_ref[...] = product(own_ref[:, mine], near_ref[...]) + product(own_ref[:, rest], far_ref[...])

        @pl.when((core == k) & jnp.logical_not(left))
        def _(mine=mine, rest=rest):
            out_ref[mine, :] = product(near_ref[...], own_ref[...])
            out_ref[rest, :] = product(far_ref[...], own_ref[...])


def level_kernel(bit, own_ref, near_ref, far_ref, out_ref, half_ref):
    combine(bit, 0, own_ref, near_ref, far_ref, out_ref)
    half_of(lax.axis_index("cuts"), out_ref, half_ref)


def last_kernel(own_ref, near_ref, far_ref, block_ref, log_ref, whole_ref):
    combine(0, 1, own_ref, near_ref, far_ref, whole_ref)
    whole = whole_ref[...]
    square = jnp.sum(jnp.sum(whole * whole, axis=0, keepdims=True), axis=1, keepdims=True)
    spread = jnp.sqrt(square / whole.size + 1e-06)
    rows, cols = block_ref.shape
    start = pl.multiple_of(lax.axis_index("tile") * rows, 8)
    core = lax.axis_index("cuts")
    for k in range(whole.shape[1] // cols):

        @pl.when(core == k)
        def _(k=k):
            block_ref[...] = whole_ref[pl.ds(start, rows), k * cols : (k + 1) * cols] / spread

    log_ref[...] = jnp.log(spread)


def product_nt(a, b):
    ah, al = split2(a)
    bh, bl = split2(b)
    last = ((1,), (1,))
    return mul(ah, bh, last) + (mul(ah, bl, last) + mul(al, bh, last))


def fold_half(flip, own_ref, other_ref, half_ref):
    core = lax.axis_index("cuts")
    side = (lax.axis_index("tile") >> 2) & 1
    size = half_ref.shape[0]
    for k in range(2):
        left, right = (own_ref, other_ref) if k else (other_ref, own_ref)
        at = slice((k ^ flip) * size, ((k ^ flip) + 1) * size)

        @pl.when((core == k) & (side == 0))
        def _(left=left, right=right, at=at):
            half_ref[...] = product(left[at, :], right[...])

        @pl.when((core == k) & (side == 1))
        def _(left=left, right=right, at=at):
            half_ref[...] = jnp.transpose(product(left[...], right[:, at]))


def fold_own_kernel(own_ref, other_ref, high_ref, low_ref, *refs):
    half_ref, parts = refs[-1], refs[:-1]
    fold_half(0, own_ref, other_ref, half_ref)
    start = 0
    for part in parts:
        part[...] = half_ref[start : start + part.shape[0], :]
        start += part.shape[0]
    high_ref[...], low_ref[...] = split2(half_ref[...])


def fold_rest_kernel(own_ref, other_ref, high_ref, low_ref, half_ref):
    fold_half(1, own_ref, other_ref, half_ref)
    high_ref[...], low_ref[...] = split2(half_ref[...])


def fold_kernel(near_ref, high_ref, low_ref, rest_high_ref, rest_low_ref, out_ref):
    core = lax.axis_index("cuts")
    size = high_ref.shape[0]
    total = None
    for at, high, low in ((core, high_ref, low_ref), (1 - core, rest_high_ref, rest_low_ref)):
        ah, al = split2(near_ref[:, pl.ds(pl.multiple_of(at * size, 128), size)])
        part = mul(ah, high[...]) + (mul(ah, low[...]) + mul(al, high[...]))
        total = part if total is None else total + part
    out_ref[...] = total


def fold_wide_kernel(*refs):
    out_ref, groups = refs[-1], refs[0]
    at, used = 0, 1
    for count in groups:
        near, pieces = refs[used][...], refs[used + 1 : used + 1 + count]
        rows = jnp.concatenate([piece[...] for piece in pieces], axis=0)
        out_ref[:, at : at + rows.shape[0]] = product_nt(near, rows)
        at += rows.shape[0]
        used += 1 + count


def gather_pieces(mine, ref, pieces):
    first, second, third = pieces
    size = ref.shape[0] // 2
    long = first.shape[0]
    body = 2 * long
    tail = size - body
    own, other = mine * size, (1 - mine) * size
    at = own
    for piece, low, high in ((first, second, 4 * long + 2 * tail), (second, second, 4 * long), (third, third, 4 * long)):
        rows = slice(at, at + piece.shape[0])
        ref[rows, own : own + body] = piece[:, 0:body]
        ref[rows, other : other + body] = piece[:, body : 2 * body]
        ref[rows, own + body : own + size] = low[:, high : high + tail]
        ref[rows, other + body : other + size] = low[:, high + tail : high + 2 * tail]
        at += piece.shape[0]


def gather_both(near, far, ref):
    core = lax.axis_index("cuts")
    for k in range(2):

        @pl.when(core == k)
        def _(k=k):
            gather_pieces(k, ref, near)
            gather_pieces(1 - k, ref, far)


def fold_ready_kernel(count, *refs):
    near, far, (high_ref, low_ref, own_ref) = refs[:count], refs[count : 2 * count], refs[2 * count :]
    gather_both(near, far, own_ref)
    high_ref[...], low_ref[...] = split2(own_ref[...])


def fold_last_kernel(count, *refs):
    high_ref, low_ref, *refs = refs
    block_ref, send_ref, got_ref, whole_ref = refs[2 * count :]
    gather_both(refs[:count], refs[count : 2 * count], got_ref)
    core, tile = lax.axis_index("cuts"), lax.axis_index("tile")
    side, column, group = (tile >> 2) & 1, tile & 1, tile >> 1

    @pl.when(side == column)
    def _():
        gh, gl = split2(got_ref[...])
        whole_ref[...] = mul(high_ref[...], gh) + (mul(high_ref[...], gl) + mul(low_ref[...], gh))

    @pl.when(side != column)
    def _():
        gh, gl = split2(got_ref[...])
        whole_ref[...] = mul(gh, high_ref[...]) + (mul(gl, high_ref[...]) + mul(gh, low_ref[...]))

    whole = whole_ref[...]
    square = jnp.sum(jnp.sum(whole * whole, axis=0, keepdims=True), axis=1, keepdims=True)
    spread = jnp.sqrt(square / whole.size + 1e-06)
    high, cols = block_ref.shape
    for ref, place in ((block_ref, group), (send_ref, group ^ 1)):
        rows_at = pl.multiple_of(place * 2 * high, 128)
        cols_at = pl.multiple_of(core * cols, 128)

        @pl.when(side == 1)
        def _(rows_at=rows_at, cols_at=cols_at):
            got_ref[0 : 2 * high, 0:cols] = whole_ref[pl.ds(rows_at, 2 * high), pl.ds(cols_at, cols)]

        @pl.when(side == 0)
        def _(rows_at=rows_at, cols_at=cols_at):
            got_ref[0 : 2 * high, 0:cols] = jnp.transpose(whole_ref[pl.ds(cols_at, cols), pl.ds(rows_at, 2 * high)])

        ref[0:high, :] = got_ref[pl.ds(pl.multiple_of(column * high, 8), high), 0:cols] / spread
    send_ref[high : high + PAD, :] = jnp.broadcast_to(jnp.log(spread), (PAD, cols))


def choose_kernel(block_ref, send_ref, got_ref, out_ref, log_ref):
    group = lax.axis_index("tile") >> 1
    inner = (group == 1) | (group == 2)
    high = out_ref.shape[0]
    out_ref[...] = jnp.where(inner, block_ref[...], got_ref[0:high, :])
    log_ref[...] = jnp.where(inner, send_ref[high : high + 1, 0:1], got_ref[high : high + 1, 0:1])


def plain_leaf(slice_rows, row_owner, leaf_row, exponent, environment, ordering, sign_mask, tiles, cap):
    width = slice_rows.shape[1]
    factor = jnp.where(exponent == -1, 0.5, jnp.where(exponent == 1, 2.0, 1.0)).astype(F32)
    scaled = slice_rows * factor[:, None]
    owners = row_owner[:, 0]
    hits = (owners[:, None] == jnp.arange(tiles, dtype=jnp.int32)[None, :]).astype(jnp.int32)
    position = jnp.sum((jnp.cumsum(hits, axis=0) - hits) * hits, axis=1)
    placed = owners * cap + position
    outgoing = jnp.zeros((tiles * cap, width), F32).at[placed].set(scaled)
    outgoing_rows = jnp.zeros((tiles * cap,), jnp.int32).at[placed].set(leaf_row)
    arrived = lax.all_to_all(outgoing, "tile", split_axis=0, concat_axis=0, tiled=True)
    arrived_rows = lax.all_to_all(outgoing_rows, "tile", split_axis=0, concat_axis=0, tiled=True)
    collected = jnp.zeros((width, width), F32).at[arrived_rows].add(arrived)
    contracted = jnp.dot(collected, environment, precision=lax.Precision.HIGHEST, preferred_element_type=F32)
    columns = jnp.arange(width, dtype=jnp.int32)
    signs = 1.0 - 2.0 * sign_mask[0].astype(F32)
    leaf = contracted + (ordering[0][:, None] == columns[None, :]).astype(F32) * signs[:, None]
    return jnp.where(native(), leaf, moved(leaf, swapped))


def packed_leaf(slice_rows, row_owner, leaf_row, exponent, environment, ordering, sign_mask, tiles, cap):
    count, width = slice_rows.shape
    sets = tiles // 2
    env = moved(environment, swapped)
    line = lambda a: a.reshape(1, count)
    outgoing = call(
        functools.partial(pack_kernel, tiles, cap),
        [like(2 * cap * (width // 128) + PAD, 128)] * sets,
        (slice_rows, line(row_owner), line(leaf_row), line(exponent), ordering, sign_mask),
        flops=6 * tiles * cap * count * width,
        held=False,
    )
    near, far = [None] * sets, [None] * sets
    ends = (0, sets - 1)
    for m in (sets - 1, 0, *range(sets - 2, 0, -1)):
        near[m] = moved(outgoing[m], routed(m, sets))
    for m in range(sets):
        far[m] = moved(near[m], other_core)
    far_own = {m: moved(outgoing[m], other_core) for m in ends}
    split = jax.ShapeDtypeStruct((width, width), BF)
    part, high, low = call(
        functools.partial(early_leaf_kernel, cap, sets),
        [like(width, width), split, split],
        (outgoing[0], outgoing[-1], environment, env, *near),
        flops=5 * width**3,
    )
    (leaf,) = call(
        functools.partial(late_leaf_kernel, cap, sets),
        [like(width, width)],
        (far_own[0], far_own[sets - 1], high, low, part, *far),
        flops=5 * width**3,
    )
    return leaf


def body(slice_rows, row_owner, leaf_row, exponent, environment, ordering, sign_mask):
    tiles = lax.axis_size("tile")
    count, width = slice_rows.shape
    cap = max(2, (3 * count + 2 * tiles - 1) // (2 * tiles))
    narrow = cap % 8 == 0 and cap <= 64 and tiles // 2 in (2, 4, 8) and width % 128 == 0 and width <= 768
    make_leaf = packed_leaf if narrow else plain_leaf
    leaf = make_leaf(slice_rows, row_owner, leaf_row, exponent, environment, ordering, sign_mask, tiles, cap)
    if tiles == 8 and width % 512 == 0:
        return center_tree(leaf, tiles, width)
    return plain_tree(leaf, tiles, width)


def center(t, c):
    return (t ^ 6, c) if t >> 1 in (1, 2) else (t, c ^ 1)


def piece_rows(size):
    long = 3 * size // 8
    return long, long, size - 2 * long


def center_tree(leaf, tiles, width):
    sizes = piece_rows(width // 2)
    count = len(sizes)
    cost = 6 * width**2
    pieces = [like(rows, width) for rows in sizes]
    half = jax.ShapeDtypeStruct((width // 2, width), BF)
    scratch = [pltpu.VMEM((width // 2, width), F32)]
    other = moved(leaf, other_core)
    high, low, *parts = call(
        fold_own_kernel, [half, half] + pieces, (leaf, other), scratch=scratch, flops=cost * width // 2
    )
    rest = call(fold_rest_kernel, [half, half], (leaf, other), scratch=scratch, flops=cost * width // 2)
    near = [moved(part, across(1)) for part in parts]
    first, first_far, got = [], [], []
    for p in range(count):
        (done,) = call(fold_kernel, [pieces[p]], (near[p], high, low, *rest), flops=cost * sizes[p])
        first.append(done)
        got.append(moved(done, center))
        first_far.append(moved(done, other_core))
    mine, mine_far, theirs = [], [], []
    long, last = first[:2] + first_far[:2], [first[2], first_far[2]]
    for p, groups in enumerate(([(0, long)], [(1, long + last), (0, last)], [(2, long + last)])):
        columns = [sum(piece.shape[0] for piece in pieces_in) for _, pieces_in in groups]
        args = [x for q, pieces_in in groups for x in (got[q], *pieces_in)]
        kernel = functools.partial(fold_wide_kernel, [len(pieces_in) for _, pieces_in in groups])
        (done,) = call(kernel, [like(sizes[p], sum(columns))], args, flops=6 * width * sizes[p] * sum(columns))
        mine.append(done)
        theirs.append(moved(done, across(0)))
        mine_far.append(moved(done, other_core))
    theirs_far = [moved(part, other_core) for part in theirs]
    tall, cols = width // tiles, width // 2
    split = jax.ShapeDtypeStruct((width, width), BF)
    own = call(
        functools.partial(fold_ready_kernel, count),
        [split, split],
        (*mine, *mine_far),
        scratch=[pltpu.VMEM((width, width), F32)],
        flops=width * width,
    )
    block, send = call(
        functools.partial(fold_last_kernel, count),
        [like(tall, cols), like(tall + PAD, cols)],
        (*own, *theirs, *theirs_far),
        scratch=[pltpu.VMEM((width, width), F32)] * 2,
        flops=cost * width,
    )
    out, log = call(
        choose_kernel, [like(tall, cols), like(1, 1)], (block, send, moved(send, across(1))), kept=False
    )
    return out, log.reshape(1)


def plain_tree(leaf, tiles, width):
    whole, half = like(width, width), like(width // 2, width)
    cost = 6 * width**3
    own, part = call(pair_kernel, [whole, half], (leaf, moved(leaf, other_core)), flops=cost)
    for level in range(1, tiles.bit_length() - 1):
        near = moved(part, across(level))
        far = moved(near, other_core)
        own, part = call(functools.partial(level_kernel, level), [whole, half], (own, near, far), flops=cost)
    near = moved(part, across(0))
    far = moved(near, other_core)
    block, log = call(
        last_kernel,
        [like(width // tiles, width // 2), like(1, 1)],
        (own, near, far),
        scratch=[pltpu.VMEM((width, width), F32)],
        flops=cost,
        kept=False,
    )
    return block, log.reshape(1)


def solution(mesh):
    return jax.shard_map(
        body,
        mesh=mesh,
        in_specs=(
            P(("groups", "tile", "cuts"), None),
            P(("groups", "tile", "cuts"), None),
            P(("groups", "tile", "cuts")),
            P(("groups", "tile", "cuts")),
            P(("groups", "tile", "cuts"), None),
            P(("groups", "tile", "cuts"), None),
            P(("groups", "tile", "cuts"), None),
        ),
        out_specs=(P(("groups", "tile"), "cuts"), P("groups")),
        check_vma=False,
    )
```

```python
import functools

import jax
import jax.numpy as jnp
from jax import lax
from jax.experimental import pallas as pl
from jax.experimental.pallas import tpu as pltpu
from jax.sharding import PartitionSpec as P


AXES = ("groups", "tile", "cuts")
VMEM = pl.BlockSpec(memory_space=pltpu.VMEM)
BF, F32 = jnp.bfloat16, jnp.float32
PAD = 8
GRANT = 16 << 20


def pairs(groups, tiles, place):
    out = []
    for g in range(groups):
        for t in range(tiles):
            for c in range(2):
                to, core, *cross = place(t, c)
                group = g ^ 1 if cross and (g ^ 1) < groups else g
                out.append(((g * tiles + t) * 2 + c, (group * tiles + to) * 2 + core))
    return out


def moved(x, place):
    return lax.ppermute(x, AXES, pairs(lax.axis_size("groups"), lax.axis_size("tile"), place))


def native():
    return (lax.axis_index("tile") & 1) != lax.axis_index("cuts")


def swapped(t, c):
    return (t ^ 1, c ^ 1) if (t & 1) == c else (t, c, True)


def turned(group, sets):
    return 3 if sets == 4 and group in (1, 2) else 0


def routed(m, sets):
    def place(t, c):
        step = m ^ turned(t >> 1, sets)
        if step == 0:
            return swapped(t, c)
        to = t ^ (step << 1)
        return (to ^ 1, c ^ 1) if (t & 1) == c else (to, c)

    return place


def is_inner(sets):
    group = lax.axis_index("tile") >> 1
    return ((group == 1) | (group == 2)) if sets == 4 else group < 0


def other_core(t, c):
    return t, c ^ 1


def across(level):
    return lambda t, c: (t ^ (1 << level), c)


def mul(a, b, dims=None):
    if dims is None:
        return jnp.dot(a, b, preferred_element_type=F32)
    return lax.dot_general(a, b, (dims, ((), ())), preferred_element_type=F32)


def split2(x):
    hi = x.astype(BF)
    return hi, (x - hi.astype(F32)).astype(BF)


def split3(x):
    hi = x.astype(BF)
    rest = x - hi.astype(F32)
    mid = rest.astype(BF)
    return hi, mid, (rest - mid.astype(F32)).astype(BF)


def product(a, b):
    ah, al = split2(a)
    bh, bl = split2(b)
    return mul(ah, bh) + (mul(ah, bl) + mul(al, bh))


def call(kernel, outs, args, scratch=(), flops=0, held=True, kept=True):
    size = sum(a.size * 4 for a in args) + sum(o.size * 4 for o in outs)
    args = [pltpu.with_memory_space_constraint(a, pltpu.VMEM if held else pltpu.HBM) for a in args]
    return pl.pallas_call(
        kernel,
        out_shape=tuple(pltpu.VMEM(o.shape, o.dtype) if kept else o for o in outs),
        in_specs=[VMEM] * len(args),
        out_specs=tuple([VMEM] * len(outs)),
        scratch_shapes=list(scratch),
        cost_estimate=pl.CostEstimate(flops=flops, bytes_accessed=size, transcendentals=0),
        compiler_params=pltpu.CompilerParams(vmem_limit_bytes=GRANT),
    )(*args)


def like(*shape):
    return jax.ShapeDtypeStruct(shape, F32)


def pack_kernel(tiles, cap, rows_ref, owner_ref, leaf_ref, exp_ref, order_ref, sign_ref, *outs):
    count = rows_ref.shape[0]
    lanes = rows_ref.shape[1] // 128
    last = lanes * 2 * cap
    tile = lax.axis_index("tile")
    own = owner_ref[...]
    hits = own == lax.broadcasted_iota(jnp.int32, (tiles, count), 0)
    earlier = lax.broadcasted_iota(jnp.int32, (count, count), 0) < lax.broadcasted_iota(jnp.int32, (count, count), 1)
    before = mul(jnp.where(hits, 1.0, 0.0).astype(BF), jnp.where(earlier, 1.0, 0.0).astype(BF))
    position = jnp.sum(jnp.where(hits, before, 0.0), axis=0, keepdims=True).astype(jnp.int32)
    flip = jnp.where(is_inner(len(outs)), 6, 0)
    placed = (own ^ tile ^ flip) * cap + position
    power = exp_ref[...]
    factor = jnp.where(power == -1, 0.5, jnp.where(power == 1, 2.0, 1.0))
    row = leaf_ref[...] + 1
    which = lax.broadcasted_iota(jnp.int32, (PAD, count), 0)
    digits = jnp.where(which == 0, row >> 4, jnp.where(which == 1, row & 15, 0)).astype(F32).astype(BF)
    hi, mid, lo = split3(rows_ref[...])
    for m, out in enumerate(outs):
        slots = lax.broadcasted_iota(jnp.int32, (2 * cap, count), 0) + m * 2 * cap
        hot = slots == placed
        pick = jnp.where(hot, factor, 0.0).astype(BF)
        rows = mul(pick, hi) + (mul(pick, mid) + mul(pick, lo))
        for j in range(lanes):
            out[j * 2 * cap : (j + 1) * 2 * cap, :] = rows[:, j * 128 : (j + 1) * 128]
        out[last : last + PAD, :] = jnp.zeros((PAD, 128), F32)
        out[last : last + PAD, 0 : 2 * cap] = mul(digits, jnp.where(hot, 1.0, 0.0).astype(BF), ((1,), (1,)))
    code = ((order_ref[...] + 1) * (1 - 2 * sign_ref[...])).astype(F32)
    for out in (outs[0], outs[-1]):
        for j in range(lanes):
            out[last + 2 + j : last + 3 + j, :] = code[:, j * 128 : (j + 1) * 128]


def spread_rows(cap, half, blocks, eh, el):
    width = eh.shape[1]
    last = width // 128 * 2 * cap
    lane = lax.broadcasted_iota(jnp.int32, (1, 128), 1)
    targets = lax.broadcasted_iota(jnp.int32, (width, 128), 0) + 1
    gap = jnp.zeros((64 - cap, width), F32)
    rows, chosen = [], []
    for first, second in zip(blocks[::2], blocks[1::2]):
        for block in (first, second):
            columns = [block[at + half * cap : at + (half + 1) * cap, :] for at in range(0, last, 2 * cap)]
            rows += [jnp.concatenate(columns, axis=1), gap]
        ends = [block[last : last + PAD, :] for block in (first, second)]
        to = [(end[0:1, :] * 16.0 + end[1:2, :]).astype(jnp.int32) for end in ends]
        at = [pltpu.roll(jnp.broadcast_to(t, (PAD, 128)), (j * 64 - half * cap) % 128, 1)[0:1, :] for j, t in enumerate(to)]
        both = jnp.where(lane < 64, jnp.where(lane < cap, at[0], 0), jnp.where(lane < 64 + cap, at[1], 0))
        chosen.append(jnp.where(targets == both, 1.0, 0.0).astype(BF))
    rh, rl = split2(jnp.concatenate(rows, axis=0))
    sh, sl = split2(mul(rh, eh) + (mul(rh, el) + mul(rl, eh)))
    pick = jnp.concatenate(chosen, axis=1)
    return mul(pick, sh) + mul(pick, sl)


def early_leaf_kernel(cap, sets, *refs):
    packed_first, packed_last, env_own_ref, env_got_ref, *refs = refs
    near, (part_ref, high_ref, low_ref) = refs[:sets], refs[sets:]
    keep, inner = native(), is_inner(sets)
    eh, el = split2(jnp.where(keep, env_own_ref[...], env_got_ref[...]))
    high_ref[...] = eh
    low_ref[...] = el
    blocks = [ref[...] for ref in near]
    blocks[0] = jnp.where(keep & jnp.logical_not(inner), packed_first[...], blocks[0])
    blocks[-1] = jnp.where(keep & inner, packed_last[...], blocks[-1])
    width = eh.shape[1]
    lanes = width // 128
    last = lanes * 2 * cap
    code = jnp.transpose(jnp.where(inner, blocks[-1][last : last + PAD, :], blocks[0][last : last + PAD, :]))
    column = jnp.concatenate([code[:, 2 + j : 3 + j] for j in range(lanes)], axis=0)
    bond = (jnp.abs(column) - 1.0).astype(jnp.int32)
    sign = jnp.where(column < 0.0, -1.0, 1.0)
    spots = lax.broadcasted_iota(jnp.int32, (width, width), 1)
    signed = jnp.where(spots == bond, sign, 0.0)
    part_ref[...] = signed + spread_rows(cap, 0, blocks, eh, el)


def late_leaf_kernel(cap, sets, *refs):
    packed_first, packed_last, high_ref, low_ref, part_ref, *refs = refs
    far, leaf_ref = refs[:sets], refs[sets]
    drop, inner = jnp.logical_not(native()), is_inner(sets)
    blocks = [ref[...] for ref in far]
    blocks[0] = jnp.where(drop & jnp.logical_not(inner), packed_first[...], blocks[0])
    blocks[-1] = jnp.where(drop & inner, packed_last[...], blocks[-1])
    leaf_ref[...] = part_ref[...] + spread_rows(cap, 1, blocks, high_ref[...], low_ref[...])


def half_of(core, value, half_ref):
    size = half_ref.shape[0]
    for k in range(2):

        @pl.when(core == k)
        def _(k=k):
            half_ref[...] = value[k * size : (k + 1) * size, :]


def pair_kernel(own_ref, other_ref, out_ref, half_ref):
    core = lax.axis_index("cuts")

    @pl.when(core == 1)
    def _():
        out_ref[...] = product(own_ref[...], other_ref[...])

    @pl.when(core == 0)
    def _():
        out_ref[...] = product(other_ref[...], own_ref[...])

    half_of(core, out_ref, half_ref)


def combine(bit, left_if, own_ref, near_ref, far_ref, out_ref):
    core = lax.axis_index("cuts")
    left = ((lax.axis_index("tile") >> bit) & 1) == left_if
    size = near_ref.shape[0]
    for k in range(2):
        mine, rest = slice(k * size, (k + 1) * size), slice((1 - k) * size, (2 - k) * size)

        @pl.when((core == k) & left)
        def _(mine=mine, rest=rest):
            out_ref[...] = product(own_ref[:, mine], near_ref[...]) + product(own_ref[:, rest], far_ref[...])

        @pl.when((core == k) & jnp.logical_not(left))
        def _(mine=mine, rest=rest):
            out_ref[mine, :] = product(near_ref[...], own_ref[...])
            out_ref[rest, :] = product(far_ref[...], own_ref[...])


def level_kernel(bit, own_ref, near_ref, far_ref, out_ref, half_ref):
    combine(bit, 0, own_ref, near_ref, far_ref, out_ref)
    half_of(lax.axis_index("cuts"), out_ref, half_ref)


def last_kernel(own_ref, near_ref, far_ref, block_ref, log_ref, whole_ref):
    combine(0, 1, own_ref, near_ref, far_ref, whole_ref)
    whole = whole_ref[...]
    square = jnp.sum(jnp.sum(whole * whole, axis=0, keepdims=True), axis=1, keepdims=True)
    spread = jnp.sqrt(square / whole.size + 1e-06)
    rows, cols = block_ref.shape
    start = pl.multiple_of(lax.axis_index("tile") * rows, 8)
    core = lax.axis_index("cuts")
    for k in range(whole.shape[1] // cols):

        @pl.when(core == k)
        def _(k=k):
            block_ref[...] = whole_ref[pl.ds(start, rows), k * cols : (k + 1) * cols] / spread

    log_ref[...] = jnp.log(spread)


def product_nt(a, b):
    ah, al = split2(a)
    bh, bl = split2(b)
    last = ((1,), (1,))
    return mul(ah, bh, last) + (mul(ah, bl, last) + mul(al, bh, last))


def fold_half(flip, own_ref, other_ref, half_ref):
    core = lax.axis_index("cuts")
    side = (lax.axis_index("tile") >> 2) & 1
    size = half_ref.shape[0]
    for k in range(2):
        left, right = (own_ref, other_ref) if k else (other_ref, own_ref)
        at = slice((k ^ flip) * size, ((k ^ flip) + 1) * size)

        @pl.when((core == k) & (side == 0))
        def _(left=left, right=right, at=at):
            half_ref[...] = product(left[at, :], right[...])

        @pl.when((core == k) & (side == 1))
        def _(left=left, right=right, at=at):
            half_ref[...] = jnp.transpose(product(left[...], right[:, at]))


def fold_own_kernel(own_ref, other_ref, high_ref, low_ref, *refs):
    half_ref, parts = refs[-1], refs[:-1]
    fold_half(0, own_ref, other_ref, half_ref)
    start = 0
    for part in parts:
        part[...] = half_ref[start : start + part.shape[0], :]
        start += part.shape[0]
    high_ref[...], low_ref[...] = split2(half_ref[...])


def fold_rest_kernel(own_ref, other_ref, high_ref, low_ref, half_ref):
    fold_half(1, own_ref, other_ref, half_ref)
    high_ref[...], low_ref[...] = split2(half_ref[...])


def fold_kernel(near_ref, high_ref, low_ref, rest_high_ref, rest_low_ref, out_ref):
    core = lax.axis_index("cuts")
    size = high_ref.shape[0]
    total = None
    for at, high, low in ((core, high_ref, low_ref), (1 - core, rest_high_ref, rest_low_ref)):
        ah, al = split2(near_ref[:, pl.ds(pl.multiple_of(at * size, 128), size)])
        part = mul(ah, high[...]) + (mul(ah, low[...]) + mul(al, high[...]))
        total = part if total is None else total + part
    out_ref[...] = total


def fold_wide_kernel(*refs):
    out_ref, groups = refs[-1], refs[0]
    at, used = 0, 1
    for count in groups:
        near, pieces = refs[used][...], refs[used + 1 : used + 1 + count]
        rows = jnp.concatenate([piece[...] for piece in pieces], axis=0)
        out_ref[:, at : at + rows.shape[0]] = product_nt(near, rows)
        at += rows.shape[0]
        used += 1 + count


def put_rows(mine, ref, at, piece, ends):
    size = ref.shape[1] // 2
    tail = 2 * size // 8
    body = size - tail
    own, other = mine * size, (1 - mine) * size
    rows = slice(at, at + piece.shape[0])
    ref[rows, own : own + body] = piece[:, 0:body]
    ref[rows, other : other + body] = piece[:, body : 2 * body]
    ends_ref, start = ends
    ref[rows, own + body : own + size] = ends_ref[:, start : start + tail]
    ref[rows, other + body : other + size] = ends_ref[:, start + tail : start + 2 * tail]


def gather_pieces(mine, ref, pieces):
    width = ref.shape[1]
    first, second = pieces[:2]
    body = width - width // 4
    at = mine * (width // 2)
    put_rows(mine, ref, at, first, (second, width))
    put_rows(mine, ref, at + first.shape[0], second, (second, body))
    for third in pieces[2:]:
        put_rows(mine, ref, at + 2 * first.shape[0], third, (third, body))


def gather_both(near, far, ref):
    core = lax.axis_index("cuts")
    for k in range(2):

        @pl.when(core == k)
        def _(k=k):
            gather_pieces(k, ref, near)
            gather_pieces(1 - k, ref, far)


def is_own_left():
    tile = lax.axis_index("tile")
    return ((tile >> 2) & 1) == (tile & 1)


def fold_ready_kernel(count, *refs):
    near, far, (high_ref, low_ref, own_ref) = refs[:count], refs[count : 2 * count], refs[2 * count :]
    gather_both(near, far, own_ref)
    high_ref[...], low_ref[...] = split2(own_ref[...])


def fold_ends_kernel(high_ref, low_ref, end_high_ref, end_low_ref):
    core = lax.axis_index("cuts")
    size = high_ref.shape[1] // 2
    tail = end_high_ref.shape[1] // 2
    for ref, end_ref in ((high_ref, end_high_ref), (low_ref, end_low_ref)):
        first, second = (ref[:, (j + 1) * size - tail : (j + 1) * size].astype(F32) for j in range(2))
        both = jnp.where(core == 0, jnp.concatenate([first, second], axis=1), jnp.concatenate([second, first], axis=1))
        end_ref[...] = both.astype(BF)


def fold_partial_kernel(high_ref, low_ref, near0, near1, far0, far1, part_ref, got_ref):
    size = got_ref.shape[0] // 2
    tail = size - 2 * near0.shape[0]
    for j in range(2):
        got_ref[(j + 1) * size - tail : (j + 1) * size, :] = jnp.zeros((tail, got_ref.shape[1]), F32)
    gather_both((near0, near1), (far0, far1), got_ref)
    left = is_own_left()

    @pl.when(left)
    def _():
        gh, gl = split2(got_ref[...])
        part_ref[...] = mul(high_ref[...], gh) + (mul(high_ref[...], gl) + mul(low_ref[...], gh))

    @pl.when(jnp.logical_not(left))
    def _():
        gh, gl = split2(got_ref[...])
        part_ref[...] = mul(gh, high_ref[...]) + (mul(gl, high_ref[...]) + mul(gh, low_ref[...]))


def fold_last_kernel(high_ref, low_ref, end_high_ref, end_low_ref, part_ref, near_ref, far_ref, *refs):
    block_ref, send_ref, got_ref, whole_ref = refs
    core, tile = lax.axis_index("cuts"), lax.axis_index("tile")
    side, column, group = (tile >> 2) & 1, tile & 1, tile >> 1
    width = whole_ref.shape[1]
    tail, size = near_ref.shape[0], width // 2
    body = width - width // 4
    for k in range(2):

        @pl.when(core == k)
        def _(k=k):
            put_rows(k, got_ref, 0, near_ref, (near_ref, body))
            put_rows(1 - k, got_ref, tail, far_ref, (far_ref, body))

    gh, gl = split2(got_ref[...])
    left = is_own_left()

    @pl.when(left)
    def _():
        more = mul(end_high_ref[...], gh) + (mul(end_high_ref[...], gl) + mul(end_low_ref[...], gh))
        whole_ref[...] = part_ref[...] + more

    @pl.when(jnp.logical_not(left))
    def _():
        rows = mul(gh, high_ref[...]) + (mul(gl, high_ref[...]) + mul(gh, low_ref[...]))
        whole_ref[...] = part_ref[...]
        for j, at in enumerate((core, 1 - core)):
            start = pl.multiple_of(at * size + size - tail, 8)
            whole_ref[pl.ds(start, tail), :] = rows[j * tail : (j + 1) * tail, :]

    whole = whole_ref[...]
    square = jnp.sum(jnp.sum(whole * whole, axis=0, keepdims=True), axis=1, keepdims=True)
    spread = jnp.sqrt(square / whole.size + 1e-06)
    high, cols = block_ref.shape
    for ref, place in ((block_ref, group), (send_ref, group ^ 1)):
        rows_at = pl.multiple_of(place * 2 * high, 128)
        cols_at = pl.multiple_of(core * cols, 128)

        @pl.when(side == 1)
        def _(rows_at=rows_at, cols_at=cols_at):
            got_ref[0 : 2 * high, 0:cols] = whole_ref[pl.ds(rows_at, 2 * high), pl.ds(cols_at, cols)]

        @pl.when(side == 0)
        def _(rows_at=rows_at, cols_at=cols_at):
            got_ref[0 : 2 * high, 0:cols] = jnp.transpose(whole_ref[pl.ds(cols_at, cols), pl.ds(rows_at, 2 * high)])

        ref[0:high, :] = got_ref[pl.ds(pl.multiple_of(column * high, 8), high), 0:cols] / spread
    send_ref[high : high + PAD, :] = jnp.broadcast_to(jnp.log(spread), (PAD, cols))


def choose_kernel(block_ref, send_ref, got_ref, out_ref, log_ref):
    group = lax.axis_index("tile") >> 1
    inner = (group == 1) | (group == 2)
    high = out_ref.shape[0]
    out_ref[...] = jnp.where(inner, block_ref[...], got_ref[0:high, :])
    log_ref[...] = jnp.where(inner, send_ref[high : high + 1, 0:1], got_ref[high : high + 1, 0:1])


def plain_leaf(slice_rows, row_owner, leaf_row, exponent, environment, ordering, sign_mask, tiles, cap):
    width = slice_rows.shape[1]
    factor = jnp.where(exponent == -1, 0.5, jnp.where(exponent == 1, 2.0, 1.0)).astype(F32)
    scaled = slice_rows * factor[:, None]
    owners = row_owner[:, 0]
    hits = (owners[:, None] == jnp.arange(tiles, dtype=jnp.int32)[None, :]).astype(jnp.int32)
    position = jnp.sum((jnp.cumsum(hits, axis=0) - hits) * hits, axis=1)
    placed = owners * cap + position
    outgoing = jnp.zeros((tiles * cap, width), F32).at[placed].set(scaled)
    outgoing_rows = jnp.zeros((tiles * cap,), jnp.int32).at[placed].set(leaf_row)
    arrived = lax.all_to_all(outgoing, "tile", split_axis=0, concat_axis=0, tiled=True)
    arrived_rows = lax.all_to_all(outgoing_rows, "tile", split_axis=0, concat_axis=0, tiled=True)
    collected = jnp.zeros((width, width), F32).at[arrived_rows].add(arrived)
    contracted = jnp.dot(collected, environment, precision=lax.Precision.HIGHEST, preferred_element_type=F32)
    columns = jnp.arange(width, dtype=jnp.int32)
    signs = 1.0 - 2.0 * sign_mask[0].astype(F32)
    leaf = contracted + (ordering[0][:, None] == columns[None, :]).astype(F32) * signs[:, None]
    return jnp.where(native(), leaf, moved(leaf, swapped))


def packed_leaf(slice_rows, row_owner, leaf_row, exponent, environment, ordering, sign_mask, tiles, cap):
    count, width = slice_rows.shape
    sets = tiles // 2
    env = moved(environment, swapped)
    line = lambda a: a.reshape(1, count)
    outgoing = call(
        functools.partial(pack_kernel, tiles, cap),
        [like(2 * cap * (width // 128) + PAD, 128)] * sets,
        (slice_rows, line(row_owner), line(leaf_row), line(exponent), ordering, sign_mask),
        flops=6 * tiles * cap * count * width,
        held=False,
    )
    near, far = [None] * sets, [None] * sets
    ends = (0, sets - 1)
    for m in (sets - 1, 0, *range(sets - 2, 0, -1)):
        near[m] = moved(outgoing[m], routed(m, sets))
    for m in range(sets):
        far[m] = moved(near[m], other_core)
    far_own = {m: moved(outgoing[m], other_core) for m in ends}
    split = jax.ShapeDtypeStruct((width, width), BF)
    part, high, low = call(
        functools.partial(early_leaf_kernel, cap, sets),
        [like(width, width), split, split],
        (outgoing[0], outgoing[-1], environment, env, *near),
        flops=5 * width**3,
    )
    (leaf,) = call(
        functools.partial(late_leaf_kernel, cap, sets),
        [like(width, width)],
        (far_own[0], far_own[sets - 1], high, low, part, *far),
        flops=5 * width**3,
    )
    return leaf


def body(slice_rows, row_owner, leaf_row, exponent, environment, ordering, sign_mask):
    tiles = lax.axis_size("tile")
    count, width = slice_rows.shape
    cap = max(2, (3 * count + 2 * tiles - 1) // (2 * tiles))
    narrow = cap % 8 == 0 and cap <= 64 and tiles // 2 in (2, 4, 8) and width % 128 == 0 and width <= 768
    make_leaf = packed_leaf if narrow else plain_leaf
    leaf = make_leaf(slice_rows, row_owner, leaf_row, exponent, environment, ordering, sign_mask, tiles, cap)
    if tiles == 8 and width % 512 == 0:
        return center_tree(leaf, tiles, width)
    return plain_tree(leaf, tiles, width)


def center(t, c):
    return (t ^ 6, c) if t >> 1 in (1, 2) else (t, c ^ 1)


def piece_rows(size):
    long = 3 * size // 8
    return long, long, size - 2 * long


def center_tree(leaf, tiles, width):
    sizes = piece_rows(width // 2)
    count = len(sizes)
    cost = 6 * width**2
    pieces = [like(rows, width) for rows in sizes]
    half = jax.ShapeDtypeStruct((width // 2, width), BF)
    scratch = [pltpu.VMEM((width // 2, width), F32)]
    other = moved(leaf, other_core)
    high, low, *parts = call(
        fold_own_kernel, [half, half] + pieces, (leaf, other), scratch=scratch, flops=cost * width // 2
    )
    rest = call(fold_rest_kernel, [half, half], (leaf, other), scratch=scratch, flops=cost * width // 2)
    near = [moved(part, across(1)) for part in parts]
    first, first_far, got = [], [], []
    for p in range(count):
        (done,) = call(fold_kernel, [pieces[p]], (near[p], high, low, *rest), flops=cost * sizes[p])
        first.append(done)
        got.append(moved(done, center))
        first_far.append(moved(done, other_core))
    mine, mine_far, theirs = [], [], []
    long, last = first[:2] + first_far[:2], [first[2], first_far[2]]
    for p, groups in enumerate(([(0, long)], [(1, long + last), (0, last)], [(2, long + last)])):
        columns = [sum(piece.shape[0] for piece in pieces_in) for _, pieces_in in groups]
        args = [x for q, pieces_in in groups for x in (got[q], *pieces_in)]
        kernel = functools.partial(fold_wide_kernel, [len(pieces_in) for _, pieces_in in groups])
        (done,) = call(kernel, [like(sizes[p], sum(columns))], args, flops=6 * width * sizes[p] * sum(columns))
        mine.append(done)
        theirs.append(moved(done, across(0)))
        mine_far.append(moved(done, other_core))
    theirs_far = [moved(part, other_core) for part in theirs]
    tall, cols = width // tiles, width // 2
    split = jax.ShapeDtypeStruct((width, width), BF)
    ends = jax.ShapeDtypeStruct((width, 2 * sizes[2]), BF)
    square = [pltpu.VMEM((width, width), F32)]
    own = call(
        functools.partial(fold_ready_kernel, count),
        [split, split],
        (*mine, *mine_far),
        scratch=square,
        flops=width * width,
    )
    own += call(fold_ends_kernel, [ends, ends], own, flops=width * width)
    (part,) = call(
        fold_partial_kernel,
        [like(width, width)],
        (*own[:2], *theirs[:2], *theirs_far[:2]),
        scratch=square,
        flops=cost * width,
    )
    block, send = call(
        fold_last_kernel,
        [like(tall, cols), like(tall + PAD, cols)],
        (*own, part, theirs[2], theirs_far[2]),
        scratch=[pltpu.VMEM((2 * sizes[2], width), F32)] + square,
        flops=cost * width // 2,
    )
    out, log = call(
        choose_kernel, [like(tall, cols), like(1, 1)], (block, send, moved(send, across(1))), kept=False
    )
    return out, log.reshape(1)


def plain_tree(leaf, tiles, width):
    whole, half = like(width, width), like(width // 2, width)
    cost = 6 * width**3
    own, part = call(pair_kernel, [whole, half], (leaf, moved(leaf, other_core)), flops=cost)
    for level in range(1, tiles.bit_length() - 1):
        near = moved(part, across(level))
        far = moved(near, other_core)
        own, part = call(functools.partial(level_kernel, level), [whole, half], (own, near, far), flops=cost)
    near = moved(part, across(0))
    far = moved(near, other_core)
    block, log = call(
        last_kernel,
        [like(width // tiles, width // 2), like(1, 1)],
        (own, near, far),
        scratch=[pltpu.VMEM((width, width), F32)],
        flops=cost,
        kept=False,
    )
    return block, log.reshape(1)


def solution(mesh):
    return jax.shard_map(
        body,
        mesh=mesh,
        in_specs=(
            P(("groups", "tile", "cuts"), None),
            P(("groups", "tile", "cuts"), None),
            P(("groups", "tile", "cuts")),
            P(("groups", "tile", "cuts")),
            P(("groups", "tile", "cuts"), None),
            P(("groups", "tile", "cuts"), None),
            P(("groups", "tile", "cuts"), None),
        ),
        out_specs=(P(("groups", "tile"), "cuts"), P("groups")),
        check_vma=False,
    )
```
